32 devices in a mesh: grp: 2 (over core), shard: 16 (over z, y, x).
Axes of the slice: x: 2, y: 2, z: 4, core: 2. Of those that a mesh axis runs over, the one named last changes fastest.
Arguments:
- tokens: bfloat16 [2, 4, 1024, 1536], P(None, 'grp', 'shard'), may hold values from -6 to 6
- lengths: int32 [2, 2, 2], P(None, 'grp'), may hold values from 1 to 1536, 2048 in all within a row
- piece_order: int32 [2, 2, 2], P(None, 'grp'), may hold values from 0 to 1, as said below
- predecessor: int32 [2, 2, 2], P(None, 'grp'), may hold values from -1 to 1, as said below
- gain_one: bfloat16 [1536], P('shard'), may hold values from 0.099609375 to 1.8984375
- query_weight: bfloat16 [1536, 1536], P('shard'), may hold values from -0.21875 to 0.21875
- keyval_weight: bfloat16 [1536, 256], P('shard'), may hold values from -0.21875 to 0.21875
- outproj_weight: bfloat16 [1536, 1536], P('shard'), may hold values from -0.875 to 0.875
- gain_two: bfloat16 [1536], P('shard'), may hold values from 0.099609375 to 1.8984375
- gate_weight: bfloat16 [1536, 4608], P('shard'), may hold values from -0.15625 to 0.15625
- up_weight: bfloat16 [1536, 4608], P('shard'), may hold values from -0.15625 to 0.15625
- down_weight: bfloat16 [4608, 1536], P('shard'), may hold values from -0.1875 to 0.1875
- cotangent: bfloat16 [2, 4, 1024, 1536], P(None, 'grp', 'shard'), may hold values from -6 to 6
Outputs:
- block_output: bfloat16 [2, 4, 1024, 1536], P(None, 'grp', 'shard')
- input_grad: bfloat16 [2, 4, 1024, 1536], P(None, 'grp', 'shard')
- gain_one_grad: float32 [1536], P('shard')
- query_weight_grad: float32 [1536, 1536], P('shard')
- keyval_weight_grad: float32 [1536, 256], P('shard')
- outproj_weight_grad: float32 [1536, 1536], P('shard')
- gain_two_grad: float32 [1536], P('shard')
- gate_weight_grad: float32 [1536, 4608], P('shard')
- up_weight_grad: float32 [1536, 4608], P('shard')
- down_weight_grad: float32 [4608, 1536], P('shard')
The draws below stay inside these ranges and needn't reach their ends.
Inputs may be any that keep to these rules, and one draw needn't show every extreme that they name: In each stream the 2 lengths sum to 2048 and the largest is at most 1536. In each stream piece_order is a permutation of the 2 pieces. predecessor[m, g, j] is the slot that holds piece piece_order[m, g, j] - 1, and -1 where piece_order[m, g, j] is 0.
All inputs are finite; a program needn't handle non-finite values.
Results may differ from the reference program's by a relative error of at most 0.018.
Values may be sent and summed in bfloat16 or wider, within the bound.
No kernel may reach another device: no remote copies, remote signals or barrier semaphores. Data moves between devices by JAX's collectives and lax.ppermute only.
A program may use at most 256 MiB of HBM per device.

```python
import math
import jax
import jax.numpy as jnp
import numpy as np
from jax import lax

D = 1536
NH = 12
HD = 128
FF = 4608
WIN = 1024
MB = 2
H = 1536
KV = 256
PIECES = 2
STREAM = 2048
MOST_LEN = 1536
SEQS = 2
N_GRP = 2


def shared_order(key):
    base = jax.random.fold_in(key, 4321)
    stream_keys = jax.random.split(base, MB * N_GRP)
    ordered = jax.vmap(lambda single: jax.random.permutation(single, PIECES))(stream_keys)
    return ordered.astype(jnp.int32)


def draw_piece_order(key, part):
    return shared_order(key).reshape(MB, N_GRP, PIECES)


def draw_predecessor(key, part):
    ordered = shared_order(key)
    places = jnp.argsort(ordered, axis=1, stable=True).astype(jnp.int32)
    earlier = jnp.maximum(ordered - 1, 0)
    slot_before = jnp.take_along_axis(places, earlier, axis=1)
    return jnp.where(ordered > 0, slot_before, -1).astype(jnp.int32).reshape(MB, N_GRP, PIECES)


def steps_of(own_key, extent, cuts, smallest, high):
    gain = 1.0
    for axis_at, blocks in cuts:
        heights = jax.random.uniform(jax.random.fold_in(jax.random.fold_in(own_key, 6), axis_at), (blocks,), jnp.float32, smallest / len(cuts), high / len(cuts))
        gain = gain * jnp.repeat(jnp.exp(heights), extent[axis_at] // blocks).reshape((-1,) + (1,) * (len(extent) - 1 - axis_at))
    return gain


def profile(amount, total, bound, slope):
    portions = [(1 << 20) // math.isqrt(rank ** slope) + 1 for rank in range(2, amount + 1)]
    spare, counts = total - bound - (amount - 1), [1] * (amount - 1)
    while spare > 0:
        movable = [i for i in range(amount - 1) if counts[i] < bound]
        pool, remaining = sum([portions[i] for i in movable]), spare
        for i in movable:
            addition = min(bound - counts[i], max(1, remaining * portions[i] // pool), spare)
            counts[i] = counts[i] + addition
            spare = spare - addition
    return np.array([bound] + counts)


def ragged_sizes(stream_key, count, total, most, slope):
    if count == 2:
        one = jax.random.randint(stream_key, (), max(1, total - most), min(most, total - 1) + 1)
        return jnp.stack([one, total - one])
    tallies = jnp.asarray(profile(count, total, most, slope), jnp.int32)
    twos = (count - 1) // 2
    source_of, receiver = tallies[1:1 + 2 * twos:2], tallies[2:2 + 2 * twos:2]
    margin = jnp.minimum(source_of - 1, most - receiver)
    shifted = jax.random.randint(jax.random.fold_in(stream_key, 1), (twos,), 0, 1 << 20) % (margin + 1)
    tallies = tallies.at[1:1 + 2 * twos:2].set(source_of - shifted).at[2:2 + 2 * twos:2].set(receiver + shifted)
    return tallies[jax.random.permutation(jax.random.fold_in(stream_key, 2), count)]


def noise(rng, shape, spread, most, shards=(), kind=jnp.bfloat16):
    values = spread * jax.random.normal(rng, shape, jnp.float32)
    if shards:
        values = values * steps_of(rng, shape, shards, -0.22, 0.18)
    return jnp.clip(values, -most, most).astype(kind)


def setup_inputs(seed: int = 0) -> dict:
    key_list = jax.random.split(jax.random.key(seed), 14)
    tokens = noise(key_list[0], (MB, N_GRP * PIECES, WIN, D), 1.0, 6.0, ((1, 2), (2, 16)))
    lengths = jax.vmap(lambda own: ragged_sizes(own, SEQS, STREAM, MOST_LEN, 2))(jax.random.split(key_list[1], MB * N_GRP)).reshape((MB, N_GRP, SEQS)).astype(jnp.int32)
    piece_order = draw_piece_order(jax.random.fold_in(key_list[13], 71), 0)
    predecessor = draw_predecessor(jax.random.fold_in(key_list[13], 71), 0)
    gain_one = jnp.clip(1.0 + 0.18 * jax.random.normal(key_list[4], (D,), jnp.float32), 0.099609375, 1.8984375).astype(jnp.bfloat16)
    query_weight = noise(key_list[5], (D, H), (D // 2) ** -0.5, 0.21875, ((0, 16),))
    keyval_weight = noise(key_list[6], (D, KV), (D // 2) ** -0.5, 0.21875, ((0, 16),))
    outproj_weight = noise(key_list[7], (H, D), (H // 32) ** -0.5, 0.875, ((0, 16),))
    gain_two = jnp.clip(1.0 + 0.18 * jax.random.normal(key_list[8], (D,), jnp.float32), 0.099609375, 1.8984375).astype(jnp.bfloat16)
    gate_weight = noise(key_list[9], (D, FF), D ** -0.5, 0.15625, ((0, 16),))
    up_weight = noise(key_list[10], (D, FF), D ** -0.5, 0.15625, ((0, 16),))
    down_weight = noise(key_list[11], (FF, D), (FF // 4) ** -0.5, 0.1875, ((0, 16),))
    cotangent = noise(key_list[12], (MB, N_GRP * PIECES, WIN, D), 1.0, 6.0, ((1, 2), (2, 16)))
    return dict(tokens=tokens, lengths=lengths, piece_order=piece_order, predecessor=predecessor, gain_one=gain_one, query_weight=query_weight, keyval_weight=keyval_weight, outproj_weight=outproj_weight, gain_two=gain_two, gate_weight=gate_weight, up_weight=up_weight, down_weight=down_weight, cotangent=cotangent)


epsilon = 1e-06
masked_out = -1e+30

@jax.custom_vjp
def low(v):
    return lax.optimization_barrier(v.astype(jnp.bfloat16)).astype(jnp.float32)

@jax.custom_vjp
def low_back(v):
    return v

def low_keep(v):
    return (low(v), None)

def low_pass(kept, grad):
    return (grad,)

def back_keep(v):
    return (v, None)

def back_low(kept, grad):
    return (low(grad),)
low.defvjp(low_keep, low_pass)
low_back.defvjp(back_keep, back_low)

def rms_factor(values):
    return lax.rsqrt(lax.optimization_barrier(jnp.mean(values * values, axis=-1, keepdims=True)) + epsilon)

def highest(first_op, second_op):
    return jnp.dot(first_op, second_op, precision=lax.Precision.HIGHEST)

def segment_of(positions, seq_ends):
    return lax.optimization_barrier(jnp.sum((positions[:, None] >= seq_ends[None, :]).astype(jnp.int32), axis=1))

def stream_layer(weights, packed):
    gain_one, query_weight, keyval_weight, outproj_weight, gain_two, gate_weight, up_weight, down_weight = weights
    stream, seq_lens, slot_piece, before = packed
    flat = stream.reshape(STREAM, D)
    normed_one = low(flat * rms_factor(flat) * gain_one)
    queries = low(low_back(highest(normed_one, query_weight)))
    keyvals = low(low_back(highest(normed_one, keyval_weight)))
    seq_ends = jnp.cumsum(seq_lens).astype(jnp.int32)
    query_blocks = queries.reshape(PIECES, WIN, NH, HD)
    keyval_blocks = keyvals.reshape(PIECES, WIN, KV)
    offsets = jnp.arange(WIN, dtype=jnp.int32)
    score_scale = 1.0 / math.sqrt(HD)

    def slot_attend(slot_idx):
        own_piece = slot_piece[slot_idx]
        has_before = before[slot_idx] >= 0
        prev_piece = slot_piece[jnp.maximum(before[slot_idx], 0)]
        query_rows = query_blocks[own_piece]
        key_rows = jnp.concatenate([keyval_blocks[own_piece], keyval_blocks[prev_piece]], axis=0)
        query_pos = own_piece * WIN + offsets
        key_pos = jnp.concatenate([own_piece * WIN + offsets, prev_piece * WIN + offsets])
        key_live = jnp.concatenate([jnp.ones((WIN,), dtype=bool), jnp.broadcast_to(has_before, (WIN,))])
        distance = query_pos[:, None] - key_pos[None, :]
        same_seq = segment_of(query_pos, seq_ends)[:, None] == segment_of(key_pos, seq_ends)[None, :]
        allowed = same_seq & (distance >= 0) & (distance < WIN) & key_live[None, :]
        scores = jnp.einsum('tnh,uh->ntu', query_rows, key_rows[:, :HD], precision=lax.Precision.HIGHEST) * score_scale
        scores = jnp.where(allowed[None], low_back(scores), masked_out)
        attn_prob = low(jax.nn.softmax(scores, axis=-1))
        mixed_rows = jnp.einsum('ntu,uh->tnh', attn_prob, key_rows[:, HD:], precision=lax.Precision.HIGHEST)
        return mixed_rows.reshape(WIN, H)
    by_slot = lax.map(jax.checkpoint(slot_attend), jnp.arange(PIECES, dtype=jnp.int32))
    piece_index = jnp.arange(PIECES, dtype=jnp.int32)
    inverse = lax.optimization_barrier(jnp.sum(jnp.where(slot_piece[None, :] == piece_index[:, None], piece_index[None, :], 0), axis=1))
    mixed = low(low_back(jnp.take(by_slot, inverse, axis=0).reshape(STREAM, H)))
    residual = flat + low_back(highest(mixed, outproj_weight))
    normed_two = low(residual * rms_factor(residual) * gain_two)
    gate_pre = low_back(highest(normed_two, gate_weight))
    up_pre = low_back(highest(normed_two, up_weight))
    hidden = low(jax.nn.gelu(gate_pre) * up_pre)
    return (residual + highest(hidden, down_weight)).reshape(PIECES, WIN, D)

def reference(tokens, lengths, piece_order, predecessor, gain_one, query_weight, keyval_weight, outproj_weight, gain_two, gate_weight, up_weight, down_weight, cotangent):
    weights = tuple((tensor.astype(jnp.float32) for tensor in (gain_one, query_weight, keyval_weight, outproj_weight, gain_two, gate_weight, up_weight, down_weight)))
    streams = tokens.astype(jnp.float32).reshape(MB * N_GRP, PIECES, WIN, D)
    seq_lens = lengths.reshape(MB * N_GRP, SEQS)
    slots = piece_order.reshape(MB * N_GRP, PIECES)
    befores = predecessor.reshape(MB * N_GRP, PIECES)
    layer_fn = jax.checkpoint(stream_layer)

    def forward(inputs, params):
        return lax.map(lambda packed: layer_fn(params, packed), (inputs, seq_lens, slots, befores))
    result, pullback = jax.vjp(forward, streams, weights)
    grad_streams, grad_weights = pullback(cotangent.astype(jnp.float32).reshape(streams.shape))
    shape_out = tokens.shape
    return (result.astype(jnp.bfloat16).reshape(shape_out), grad_streams.astype(jnp.bfloat16).reshape(shape_out), grad_weights[0], grad_weights[1], grad_weights[2], grad_weights[3], grad_weights[4], grad_weights[5], grad_weights[6], grad_weights[7])
```

```python
import functools
import math

import jax
import jax.numpy as jnp
from jax import lax
from jax.experimental import pallas as pl
from jax.experimental.pallas import tpu as pltpu
from jax.sharding import PartitionSpec as P

epsilon = 1e-06
masked_out = -1e30
bf16 = jnp.bfloat16
f32 = jnp.float32
plane = 4
ring_order = (0, 1, 3, 2)


def rms_factor(values):
    return lax.rsqrt(jnp.mean(values * values, axis=-1, keepdims=True) + epsilon)


def product(first_op, second_op):
    return jnp.dot(first_op, second_op, preferred_element_type=f32)


def product_tn(first_op, second_op):
    return lax.dot_general(
        first_op, second_op, (((0,), (0,)), ((), ())), preferred_element_type=f32
    )


def product_nt(first_op, second_op):
    return lax.dot_general(
        first_op, second_op, (((1,), (1,)), ((), ())), preferred_element_type=f32
    )


def norm_backward(values, factor, gain, upstream):
    inner_mean = jnp.mean(gain * upstream * values, axis=-1, keepdims=True)
    return factor * gain * upstream - values * factor * factor * factor * inner_mean


def across(value, mask):
    count = lax.axis_size("shard")
    return lax.ppermute(value, "shard", [(i, i ^ mask) for i in range(count)])


def peer(value):
    count = lax.axis_size("grp")
    return lax.ppermute(value, "grp", [(i, i ^ 1) for i in range(count)])


def column_groups():
    count = lax.axis_size("shard")
    return [[a * plane + b for a in range(count // plane)] for b in range(plane)]


def gather_column(value):
    return lax.all_gather(
        value, "shard", axis=0, tiled=True, axis_index_groups=column_groups()
    )


def scatter_column(value):
    return lax.psum_scatter(
        value, "shard", scatter_dimension=0, tiled=True, axis_index_groups=column_groups()
    )


def gather_plane(value):
    half = value.shape[0] // 2
    first = across(value, 1)
    second = across(value, 2)
    far_top = across(first[:half], 2)
    far_bottom = across(second[half:], 1)
    return value, first, second, far_top, far_bottom


def place_plane(blocks, my_place):
    own, first, second, far_top, far_bottom = blocks
    lead, rows, width = own.shape
    out = jnp.zeros((lead, plane, rows, width), own.dtype)
    far = jnp.concatenate([far_top, far_bottom], axis=0)
    for mask, block in enumerate((own, first, second, far)):
        out = lax.dynamic_update_slice_in_dim(out, block[:, None], my_place ^ mask, axis=1)
    return out


def reduce_plane(x_send, x_keep, y_send, y_keep):
    x_got = across(x_send.astype(bf16), 1).astype(f32)
    y_got = across(y_send.astype(bf16), 2).astype(f32)
    x_last = across((x_keep[1].astype(f32) + x_got[1]).astype(bf16), 2).astype(f32)
    y_last = across((y_keep[1].astype(f32) + y_got[1]).astype(bf16), 1).astype(f32)
    return (
        x_keep[0].astype(f32) + x_got[0] + x_last,
        y_keep[0].astype(f32) + y_got[0] + y_last,
    )


def pick(stack, index):
    return lax.dynamic_index_in_dim(stack, index, axis=1, keepdims=False)


def reduce_rows(grad, my_place):
    count = lax.axis_size("shard")
    rows = grad.shape[0] // count
    lead = count // plane
    blocks = grad.reshape(lead, plane, rows, -1)
    parts = [pick(blocks, my_place ^ mask) for mask in range(plane)]
    half = lead // 2
    top = [part[:half] for part in parts]
    low = [part[half:] for part in parts]
    x_sum, y_sum = reduce_plane(
        jnp.stack([top[1], top[3]]),
        jnp.stack([top[0], top[2]]),
        jnp.stack([low[2], low[3]]),
        jnp.stack([low[0], low[1]]),
    )
    summed = jnp.concatenate([x_sum, y_sum], axis=0).astype(bf16)
    return scatter_column(summed.reshape(lead * rows, -1))


def window_mask(info, dims, micro, piece):
    sub, window, keys, pad, seqs = dims
    base = piece * window + info[1] * sub
    query = base + lax.broadcasted_iota(jnp.int32, (sub, 1), 0)
    start = jnp.zeros((sub, 1), jnp.int32)
    end = jnp.int32(0)
    for k in range(seqs - 1):
        end = end + info[2 + micro * seqs + k]
        start = jnp.where(query >= end, end, start)
    lowest = jnp.maximum(start, query - (window - 1))
    key = base - pad + lax.broadcasted_iota(jnp.int32, (sub, keys), 1)
    return jnp.where((key >= lowest) & (key <= query), 0.0, masked_out).astype(f32)


def fill_window(info, dims, micro_count, pieces, blocks, key_all, value_all):
    sub, window, keys, pad, seqs = dims
    head_size = key_all.shape[-1]
    key_all[:, :pad, :] = jnp.zeros((micro_count, pad, head_size), bf16)
    value_all[:, :pad, :] = jnp.zeros((micro_count, pad, head_size), bf16)
    slots = micro_count * pieces
    offset = {0: 0, 1: 0, 2: 0, 3: 0}
    for mask, block in zip((0, 1, 2, 3, 3), blocks):
        member = info[0] ^ mask
        first = offset[mask]
        amount = block.shape[0] // sub

        def copy(step, carry, block=block, member=member, first=first):
            index = step + first
            row = pl.multiple_of(
                pad + (index % pieces) * window + ((index // slots) * plane + member) * sub, 16
            )
            micro = (index // pieces) % micro_count
            rows = block[pl.ds(pl.multiple_of(step * sub, 16), sub), :]
            key_all[micro, pl.ds(row, sub), :] = rows[:, :head_size]
            value_all[micro, pl.ds(row, sub), :] = rows[:, head_size:]
            return carry

        lax.fori_loop(0, amount, copy, 0)
        offset[mask] = first + amount


def stack_heads(ref, rows, heads, head_size):
    block = ref[rows, :]
    return jnp.concatenate(
        [block[:, h * head_size : (h + 1) * head_size] for h in heads], axis=0
    )


def attend_forward_kernel(
    dims, micro_count, pieces, group, info, q_ref, k0, k1, k2, k3, k4, o_ref, lse_ref, key_all, value_all
):
    sub, window, keys, pad, seqs = dims
    head_size = key_all.shape[-1]
    head_count = q_ref.shape[1] // head_size
    fill_window(info, dims, micro_count, pieces, (k0, k1, k2, k3, k4), key_all, value_all)
    scale = 1.0 / math.sqrt(head_size) / math.log(2.0)

    def slot(index, carry):
        micro = index // pieces
        piece = index % pieces
        bias = window_mask(info, dims, micro, piece)
        start = pl.multiple_of(piece * window + info[1] * sub, 16)
        key_part = key_all[micro, pl.ds(start, keys), :]
        value_part = value_all[micro, pl.ds(start, keys), :]
        rows = pl.ds(pl.multiple_of(index * sub, 16), sub)
        for first in range(0, head_count, group):
            heads = range(first, first + group)
            queries = stack_heads(q_ref, rows, heads, head_size)
            scores = product_nt(queries, key_part) * scale
            scores = scores.reshape(group, sub, keys) + bias[None]
            scores = scores.reshape(group * sub, keys)
            top = jnp.max(scores, axis=-1, keepdims=True)
            weights = jnp.exp2(scores - top)
            total = jnp.sum(weights, axis=-1, keepdims=True)
            mixed = (product(weights.astype(bf16), value_part) / total).astype(bf16)
            for at, h in enumerate(heads):
                o_ref[rows, h * head_size : (h + 1) * head_size] = mixed[at * sub : (at + 1) * sub]
            lse_ref[index, first * sub : (first + group) * sub, :] = top + jnp.log2(total)
        return carry

    lax.fori_loop(0, micro_count * pieces, slot, 0)


def attend_backward_kernel(
    dims,
    micro_count,
    pieces,
    group,
    info,
    q_ref,
    g_ref,
    lse_ref,
    k0,
    k1,
    k2,
    k3,
    k4,
    dq_ref,
    kx_send,
    kx_keep,
    vy_send,
    vy_keep,
    key_all,
    value_all,
    dkey_all,
    dvalue_all,
):
    sub, window, keys, pad, seqs = dims
    head_size = key_all.shape[-1]
    head_count = q_ref.shape[1] // head_size
    fill_window(info, dims, micro_count, pieces, (k0, k1, k2, k3, k4), key_all, value_all)
    dkey_all[...] = jnp.zeros(dkey_all.shape, f32)
    dvalue_all[...] = jnp.zeros(dvalue_all.shape, f32)
    plain = 1.0 / math.sqrt(head_size)
    scale = plain / math.log(2.0)

    def slot(index, carry):
        micro = index // pieces
        piece = index % pieces
        bias = window_mask(info, dims, micro, piece)
        start = pl.multiple_of(piece * window + info[1] * sub, 16)
        key_part = key_all[micro, pl.ds(start, keys), :]
        value_part = value_all[micro, pl.ds(start, keys), :]
        rows = pl.ds(pl.multiple_of(index * sub, 16), sub)
        dkey = jnp.zeros((keys, head_size), f32)
        dvalue = jnp.zeros((keys, head_size), f32)
        for first in range(0, head_count, group):
            heads = range(first, first + group)
            queries = stack_heads(q_ref, rows, heads, head_size)
            grads = stack_heads(g_ref, rows, heads, head_size)
            lse = lse_ref[index, first * sub : (first + group) * sub, :]
            scores = product_nt(queries, key_part) * scale
            scores = scores.reshape(group, sub, keys) + bias[None]
            prob = jnp.exp2(scores.reshape(group * sub, keys) - lse)
            dprob = product_nt(grads, value_part)
            delta = jnp.sum(prob * dprob, axis=-1, keepdims=True)
            dscore = (prob * (dprob - delta)).astype(bf16)
            dquery = (product(dscore, key_part) * plain).astype(bf16)
            for at, h in enumerate(heads):
                dq_ref[rows, h * head_size : (h + 1) * head_size] = dquery[
                    at * sub : (at + 1) * sub
                ]
            dkey = dkey + product_tn(dscore, queries)
            dvalue = dvalue + product_tn(prob.astype(bf16), grads)
        dkey_all[micro, pl.ds(start, keys), :] += dkey * plain
        dvalue_all[micro, pl.ds(start, keys), :] += dvalue
        return carry

    lax.fori_loop(0, micro_count * pieces, slot, 0)
    slots = micro_count * pieces
    for mask, k_out, k_at, v_out, v_at in (
        (0, kx_keep, 0, vy_keep, 0),
        (1, kx_send, 0, vy_keep, 1),
        (2, kx_keep, 1, vy_send, 0),
        (3, kx_send, 1, vy_send, 1),
    ):
        member = info[0] ^ mask

        def copy(index, carry, member=member, k_out=k_out, k_at=k_at, v_out=v_out, v_at=v_at):
            row = pl.multiple_of(
                pad + (index % pieces) * window + ((index // slots) * plane + member) * sub, 16
            )
            micro = (index // pieces) % micro_count
            to = pl.ds(pl.multiple_of(index * sub, 16), sub)
            k_out[k_at, to, :] = dkey_all[micro, pl.ds(row, sub), :].astype(bf16)
            v_out[v_at, to, :] = dvalue_all[micro, pl.ds(row, sub), :].astype(bf16)
            return carry

        lax.fori_loop(0, kx_keep.shape[1] // sub, copy, 0)


def attention_calls(micro_count, pieces, sub, window, head_size, head_count, seqs, kv_rows):
    keys = -(-(window + sub) // 128) * 128
    pad = keys - sub
    dims = (sub, window, keys, pad, seqs)
    group = max(g for g in range(1, head_count + 1) if head_count % g == 0 and g * sub <= max(384, sub))
    token_count = micro_count * pieces * sub
    width = head_count * head_size
    smem = pl.BlockSpec(memory_space=pltpu.SMEM)
    vmem = pl.BlockSpec(memory_space=pltpu.VMEM)
    shape = jax.ShapeDtypeStruct
    span = pad + pieces * window
    work = token_count * head_count * keys
    lse_shape = shape((micro_count * pieces, head_count * sub, 1), f32)
    params = pltpu.CompilerParams(vmem_limit_bytes=56 * 2**20)
    forward = pl.pallas_call(
        functools.partial(attend_forward_kernel, dims, micro_count, pieces, group),
        out_shape=(shape((token_count, width), bf16), lse_shape),
        in_specs=[smem] + [vmem] * 6,
        out_specs=(vmem, vmem),
        scratch_shapes=[pltpu.VMEM((micro_count, span, head_size), bf16)] * 2,
        cost_estimate=pl.CostEstimate(
            flops=4 * work * head_size, transcendentals=work, bytes_accessed=4 * 2**20
        ),
        compiler_params=params,
        name="attend_forward",
    )
    block = shape((2, kv_rows, head_size), bf16)
    backward = pl.pallas_call(
        functools.partial(attend_backward_kernel, dims, micro_count, pieces, group),
        out_shape=(shape((token_count, width), bf16), block, block, block, block),
        in_specs=[smem] + [vmem] * 8,
        out_specs=(vmem,) * 5,
        scratch_shapes=[pltpu.VMEM((micro_count, span, head_size), bf16)] * 2
        + [pltpu.VMEM((micro_count, span, head_size), f32)] * 2,
        cost_estimate=pl.CostEstimate(
            flops=10 * work * head_size, transcendentals=work, bytes_accessed=8 * 2**20
        ),
        compiler_params=params,
        name="attend_backward",
    )
    return forward, backward


def on_device(
    tokens,
    lengths,
    piece_order,
    predecessor,
    gain_one,
    query_weight,
    keyval_weight,
    outproj_weight,
    gain_two,
    gate_weight,
    up_weight,
    down_weight,
    cotangent,
):
    shard_count = lax.axis_size("shard")
    grp_count = lax.axis_size("grp")
    lead = shard_count // plane
    micro_count, piece_count, sub_rows, feat = tokens.shape
    window = sub_rows * shard_count
    token_count = micro_count * piece_count * sub_rows
    head_size = keyval_weight.shape[1] // 2
    width = query_weight.shape[1]
    head_count = width // head_size
    hidden_width = gate_weight.shape[1]
    my_rows = query_weight.shape[0]
    my_hidden = down_weight.shape[0]
    part = hidden_width // plane
    half_w = width // 2
    half_d = feat // 2
    my_index = lax.axis_index("shard")
    my_place = my_index % plane
    core = lax.axis_index("grp") % 2
    first_core = core == 0

    def in_order(own, other):
        return jnp.where(
            first_core,
            jnp.concatenate([own, other], axis=1),
            jnp.concatenate([other, own], axis=1),
        )

    def halves(value):
        size = value.shape[1] // 2
        return (
            lax.dynamic_slice_in_dim(value, core * size, size, 1),
            lax.dynamic_slice_in_dim(value, (1 - core) * size, size, 1),
        )

    gain_cols = jnp.pad(jnp.stack([gain_one, gain_two], axis=1), ((0, 0), (0, 126)))
    qkv_mine = jnp.concatenate(
        [halves(query_weight)[0], halves(keyval_weight)[0], gain_cols], axis=1
    )
    out_mine = halves(outproj_weight)[0]
    attn_w = gather_column(jnp.concatenate([qkv_mine, out_mine], axis=1))
    attn_blocks = gather_plane(attn_w.reshape(lead, my_rows, -1))
    attn_own = place_plane(attn_blocks, my_place).reshape(feat, -1)
    attn_other = peer(attn_own)
    cut = half_w + head_size
    qkv_own, qkv_other = attn_own[:, :cut], attn_other[:, :cut]
    out_own, out_other = attn_own[:, cut + 128 :], attn_other[:, cut + 128 :]
    gains = attn_own[:, cut : cut + 2].T
    full_gain_one = gains[0].astype(f32)
    full_gain_two = gains[1].astype(f32)

    gate_or_up = jnp.where(first_core, gate_weight, up_weight)
    pieces_out = jnp.transpose(
        gate_or_up.reshape(my_rows, lead, plane, my_hidden), (2, 0, 1, 3)
    ).reshape(plane, my_rows, part)
    wide_in = jnp.zeros((plane, my_rows, part), bf16)
    for mask in range(plane):
        block = lax.dynamic_index_in_dim(pieces_out, my_place ^ mask, axis=0, keepdims=True)
        block = block if mask == 0 else across(block, mask)
        wide_in = lax.dynamic_update_slice_in_dim(wide_in, block, my_place ^ mask, axis=0)
    wide_own = gather_column(wide_in.reshape(plane * my_rows, part))
    down_own = gather_column(halves(down_weight)[0])
    wide_other = peer(wide_own)
    down_other = peer(down_own)

    stream = tokens.reshape(token_count, feat).astype(f32)
    factor_one = rms_factor(stream)
    normed_one = (stream * factor_one * full_gain_one).astype(bf16)
    mixed_own = product(normed_one, qkv_own).astype(bf16)
    mixed_other = product(normed_one, qkv_other).astype(bf16)
    queries = in_order(mixed_own[:, :half_w], mixed_other[:, :half_w])
    keyvals = in_order(mixed_own[:, half_w:], mixed_other[:, half_w:])
    kv_blocks = gather_plane(gather_column(keyvals))
    forward, backward = attention_calls(
        micro_count,
        piece_count,
        sub_rows,
        window,
        head_size,
        head_count,
        lengths.shape[-1],
        lead * token_count,
    )
    info = jnp.concatenate(
        [
            jnp.stack([my_place, my_index]).astype(jnp.int32),
            lengths.reshape(-1).astype(jnp.int32),
        ]
    )
    attended, logsum = forward(info, queries, *kv_blocks)
    residual = stream + in_order(product(attended, out_own), product(attended, out_other))
    factor_two = rms_factor(residual)
    normed_two = (residual * factor_two * full_gain_two).astype(bf16)

    def plane_tokens(value):
        own, first, second, far_top, far_bottom = gather_plane(value)
        return jnp.concatenate([own, first, far_top, far_bottom, second], axis=0)

    upstream = cotangent.reshape(token_count, feat)
    all_up = plane_tokens(upstream)
    all_normed = plane_tokens(normed_two)
    pre_own = product(all_normed, wide_own)
    pre_other = product(all_normed, wide_other)
    gate_pre = jnp.where(first_core, pre_own, pre_other)
    upward = jnp.where(first_core, pre_other, pre_own)
    root = math.sqrt(2.0 / math.pi)
    curve = jnp.tanh(root * (gate_pre + 0.044715 * gate_pre * gate_pre * gate_pre))
    active = 0.5 * gate_pre * (1.0 + curve)
    slope = 0.5 * (1.0 + curve) + 0.5 * gate_pre * (1.0 - curve * curve) * root * (
        1.0 + 3 * 0.044715 * gate_pre * gate_pre
    )
    hidden = (active * upward).astype(bf16)
    up_own, up_other = halves(all_up)
    grad_hidden = product_nt(up_own, down_own) + product_nt(up_other, down_other)
    grad_gate_in = (grad_hidden * upward * slope).astype(bf16)
    grad_up_in = (grad_hidden * active).astype(bf16)
    grad_own_in = jnp.where(first_core, grad_gate_in, grad_up_in)
    grad_other_in = jnp.where(first_core, grad_up_in, grad_gate_in)

    def token_sum(first_half, second_half):
        one = first_half.astype(bf16).reshape(plane, token_count, -1)
        two = second_half.astype(bf16).reshape(plane, token_count, -1)
        return reduce_plane(
            one[1:3], (one[0], one[3]), jnp.stack([two[3], two[2]]), (two[0], two[1])
        )

    out_sum = token_sum(product(hidden, down_own), product(hidden, down_other))
    block_output = (residual + in_order(*out_sum)).astype(bf16).reshape(tokens.shape)
    grad_wide = product_nt(grad_own_in, wide_own) + product_nt(grad_other_in, wide_other)
    grad_normed_two = jnp.concatenate(
        token_sum(grad_wide[:, :half_d], grad_wide[:, half_d:]), axis=1
    )

    def chip_sum(own, other):
        return (own + peer(other.astype(bf16)).astype(f32)).astype(bf16)

    down_grad = scatter_column(
        chip_sum(product_tn(hidden, up_own), product_tn(hidden, up_other))
    )
    wide_grad = scatter_column(
        chip_sum(product_tn(all_normed, grad_own_in), product_tn(all_normed, grad_other_in))
    ).reshape(plane, my_rows, part)
    wide_back = jnp.zeros((plane, my_rows, part), bf16)
    for mask in range(plane):
        block = lax.dynamic_index_in_dim(wide_grad, my_place ^ mask, axis=0, keepdims=True)
        block = block if mask == 0 else across(block, mask)
        wide_back = lax.dynamic_update_slice_in_dim(wide_back, block, my_place ^ mask, axis=0)
    wide_share = jnp.transpose(
        wide_back.reshape(plane, my_rows, lead, my_hidden), (1, 2, 0, 3)
    ).reshape(my_rows, hidden_width)

    grad_gain_two = jnp.sum(grad_normed_two * residual * factor_two, axis=0)
    grad_resid = upstream.astype(f32) + norm_backward(
        residual, factor_two, full_gain_two, grad_normed_two
    )
    grad_attn = grad_resid.astype(bf16)
    attn_own_half, attn_other_half = halves(grad_attn)
    outproj_share = reduce_rows(
        chip_sum(product_tn(attended, attn_own_half), product_tn(attended, attn_other_half)),
        my_place,
    )
    grad_mixed = (
        product_nt(attn_own_half, out_own) + product_nt(attn_other_half, out_other)
    ).astype(bf16)
    grad_queries, kx_send, kx_keep, vy_send, vy_keep = backward(
        info, queries, grad_mixed, logsum, *kv_blocks
    )
    grad_kv = jnp.concatenate(reduce_plane(kx_send, kx_keep, vy_send, vy_keep), axis=1)
    grad_keyvals = scatter_column(grad_kv.astype(bf16))
    dq_own, dq_other = halves(grad_queries)
    dkv_own, dkv_other = halves(grad_keyvals)
    query_share = reduce_rows(
        chip_sum(product_tn(normed_one, dq_own), product_tn(normed_one, dq_other)), my_place
    )
    dqkv_own = jnp.concatenate([dq_own, dkv_own], axis=1)
    dqkv_other = jnp.concatenate([dq_other, dkv_other], axis=1)
    grad_normed_one = product_nt(dqkv_own, qkv_own) + product_nt(dqkv_other, qkv_other)
    grad_gain_one = jnp.sum(grad_normed_one * stream * factor_one, axis=0)
    grad_stream = grad_resid + norm_backward(stream, factor_one, full_gain_one, grad_normed_one)
    input_grad = grad_stream.astype(bf16).reshape(tokens.shape)

    def as_column(value):
        return jnp.broadcast_to(value[:, None], (feat, 128))

    gain_own = as_column(jnp.where(first_core, grad_gain_one, grad_gain_two))
    gain_other = as_column(jnp.where(first_core, grad_gain_two, grad_gain_one))
    last_share = reduce_rows(
        chip_sum(
            jnp.concatenate([product_tn(normed_one, dkv_own), gain_own], axis=1),
            jnp.concatenate([product_tn(normed_one, dkv_other), gain_other], axis=1),
        ),
        my_place,
    )

    def whole(share):
        total = share
        for step in range(1, grp_count // 2):
            moved = lax.ppermute(
                share, "grp", [(i, (i + 2 * step) % grp_count) for i in range(grp_count)]
            )
            total = total.astype(f32) + moved.astype(f32)
        total = total.astype(bf16)
        return total.astype(f32), peer(total).astype(f32)

    wide_one, wide_two = whole(wide_share)
    down_pair = whole(down_grad)
    out_pair = whole(outproj_share)
    query_pair = whole(query_share)
    last_one, last_two = whole(last_share)
    return (
        block_output,
        input_grad,
        jnp.where(first_core, last_one[:, head_size], last_two[:, head_size]),
        in_order(*query_pair),
        in_order(last_one[:, :head_size], last_two[:, :head_size]),
        in_order(*out_pair),
        jnp.where(first_core, last_two[:, head_size], last_one[:, head_size]),
        jnp.where(first_core, wide_one, wide_two),
        jnp.where(first_core, wide_two, wide_one),
        in_order(*down_pair),
    )


def solution(mesh):
    in_specs = (
        P(None, "grp", "shard", None),
        P(None, "grp", None),
        P(None, "grp", None),
        P(None, "grp", None),
        P("shard"),
        P("shard", None),
        P("shard", None),
        P("shard", None),
        P("shard"),
        P("shard", None),
        P("shard", None),
        P("shard", None),
        P(None, "grp", "shard", None),
    )
    out_specs = (
        P(None, "grp", "shard", None),
        P(None, "grp", "shard", None),
        P("shard"),
        P("shard", None),
        P("shard", None),
        P("shard", None),
        P("shard"),
        P("shard", None),
        P("shard", None),
        P("shard", None),
    )
    return jax.shard_map(
        on_device, mesh=mesh, in_specs=in_specs, out_specs=out_specs, check_vma=False
    )
```

```python
import functools
import math

import jax
import jax.numpy as jnp
from jax import lax
from jax.experimental import pallas as pl
from jax.experimental.pallas import tpu as pltpu
from jax.sharding import PartitionSpec as P

epsilon = 1e-06
masked_out = -1e30
bf16 = jnp.bfloat16
f32 = jnp.float32
plane = 4
ring_order = (0, 1, 3, 2)


def rms_factor(values):
    return lax.rsqrt(jnp.mean(values * values, axis=-1, keepdims=True) + epsilon)


def product(first_op, second_op):
    return jnp.dot(first_op, second_op, preferred_element_type=f32)


def product_tn(first_op, second_op):
    return lax.dot_general(
        first_op, second_op, (((0,), (0,)), ((), ())), preferred_element_type=f32
    )


def product_nt(first_op, second_op):
    return lax.dot_general(
        first_op, second_op, (((1,), (1,)), ((), ())), preferred_element_type=f32
    )


def norm_backward(values, factor, gain, upstream):
    inner_mean = jnp.mean(gain * upstream * values, axis=-1, keepdims=True)
    return factor * gain * upstream - values * factor * factor * factor * inner_mean


def tie(*values):
    return lax.optimization_barrier(values)


def across(value, mask):
    count = lax.axis_size("shard")
    return lax.ppermute(value, "shard", [(i, i ^ mask) for i in range(count)])


def peer(value):
    count = lax.axis_size("grp")
    return lax.ppermute(value, "grp", [(i, i ^ 1) for i in range(count)])


def column_groups():
    count = lax.axis_size("shard")
    return [[a * plane + b for a in range(count // plane)] for b in range(plane)]


def gather_column(value):
    return lax.all_gather(
        value, "shard", axis=0, tiled=True, axis_index_groups=column_groups()
    )


def scatter_column(value):
    return lax.psum_scatter(
        value, "shard", scatter_dimension=0, tiled=True, axis_index_groups=column_groups()
    )


def halve_column(value, line_place, during=()):
    during = list(during)
    lead = lax.axis_size("shard") // plane
    held = value.reshape(lead, -1, value.shape[1])
    size = lead // 2
    done = 0
    while size >= 1:
        pair = held.reshape(2, size, *held.shape[1:])
        mine = (line_place // size) % 2
        kept = lax.dynamic_index_in_dim(pair, mine, axis=0, keepdims=False)
        got = across(
            lax.dynamic_index_in_dim(pair, 1 - mine, axis=0, keepdims=False), size * plane
        )
        if done < len(during):
            got, *during[done] = tie(got, *during[done])
            done += 1
        held = (kept.astype(f32) + got.astype(f32)).astype(bf16)
        size //= 2
    return held[0], during


def start_plane(value):
    return across(value, 1), across(value, 2)


def finish_plane(value, first, second):
    half = value.shape[0] // 2
    far_top = across(first[:half], 2)
    far_bottom = across(second[half:], 1)
    return value, first, second, far_top, far_bottom


def gather_plane(value):
    return finish_plane(value, *tie(*start_plane(value)))


def place_kernel(place, own, first, second, far_top, far_bottom, out):
    half = far_top.shape[0]
    me = place[0]
    out[:, pl.ds(me, 1)] = own[...][:, None]
    out[:, pl.ds(me ^ 1, 1)] = first[...][:, None]
    out[:, pl.ds(me ^ 2, 1)] = second[...][:, None]
    out[:half, pl.ds(me ^ 3, 1)] = far_top[...][:, None]
    out[half:, pl.ds(me ^ 3, 1)] = far_bottom[...][:, None]


def place_plane(blocks, place):
    lead, rows, width = blocks[0].shape
    vmem = pl.BlockSpec(memory_space=pltpu.VMEM)
    return pl.pallas_call(
        place_kernel,
        out_shape=jax.ShapeDtypeStruct((lead, plane, rows, width), blocks[0].dtype),
        in_specs=[pl.BlockSpec(memory_space=pltpu.SMEM)] + [vmem] * 5,
        out_specs=vmem,
        cost_estimate=pl.CostEstimate(
            flops=0, transcendentals=0, bytes_accessed=4 * plane * lead * rows * width
        ),
        name="place_plane",
    )(place, *blocks)


def unshuffle(pieces, place, unit):
    rows, part = pieces[0].shape
    lead = part // unit
    vmem = pl.BlockSpec(memory_space=pltpu.VMEM)

    def kernel(place, p0, p1, p2, p3, out, natural):
        for mask, piece in enumerate((p0, p1, p2, p3)):
            natural[pl.ds(place[0] ^ mask, 1)] = piece[...].astype(f32)[None]
        columns = [
            natural[member][:, a * unit : (a + 1) * unit]
            for a in range(lead)
            for member in range(plane)
        ]
        out[...] = jnp.concatenate(columns, axis=1).astype(bf16)

    return pl.pallas_call(
        kernel,
        out_shape=jax.ShapeDtypeStruct((rows, plane * part), bf16),
        in_specs=[pl.BlockSpec(memory_space=pltpu.SMEM)] + [vmem] * 4,
        out_specs=vmem,
        scratch_shapes=[pltpu.VMEM((plane, rows, part), f32)],
        cost_estimate=pl.CostEstimate(
            flops=0, transcendentals=0, bytes_accessed=4 * plane * rows * part
        ),
        name="unshuffle",
    )(place, *pieces)


def exchange_plane(x_send, x_keep, y_send, y_keep, during_first=(), during_second=()):
    x_got = across(x_send.astype(bf16), 1)
    y_got = across(y_send.astype(bf16), 2)
    x_got, y_got, *during_first = tie(x_got, y_got, *during_first)
    x_pass, y_pass = tie(
        (x_keep[1].astype(f32) + x_got[1].astype(f32)).astype(bf16),
        (y_keep[1].astype(f32) + y_got[0].astype(f32)).astype(bf16),
    )
    x_last = across(x_pass, 2)
    y_last = across(y_pass, 1)
    x_last, y_last, *during_second = tie(x_last, y_last, *during_second)
    return x_got, x_last, y_got, y_last, during_first, during_second


def split_kernel(place, own, got, x_send, x_keep, y_send, y_keep):
    half = own.shape[0] // 2
    for out, slot, mask, first in (
        (x_send, 0, 1, 0),
        (x_send, 1, 3, 0),
        (x_keep, 0, 0, 0),
        (x_keep, 1, 2, 0),
        (y_send, 0, 3, half),
        (y_send, 1, 2, half),
        (y_keep, 0, 0, half),
        (y_keep, 1, 1, half),
    ):
        at = (slice(first, first + half), pl.ds(place[0] ^ mask, 1))
        out[slot] = (own[at].astype(f32) + got[at].astype(f32))[:, 0].astype(bf16)


def split_rows(place, own, got, rows):
    lead = own.shape[0] // (plane * rows)
    shape = (lead, plane, rows, own.shape[1])
    vmem = pl.BlockSpec(memory_space=pltpu.VMEM)
    sent = jax.ShapeDtypeStruct((2, lead // 2, rows, own.shape[1]), bf16)
    return pl.pallas_call(
        split_kernel,
        out_shape=(sent,) * 4,
        in_specs=[pl.BlockSpec(memory_space=pltpu.SMEM), vmem, vmem],
        out_specs=(vmem,) * 4,
        cost_estimate=pl.CostEstimate(
            flops=own.size, transcendentals=0, bytes_accessed=6 * own.size
        ),
        compiler_params=pltpu.CompilerParams(vmem_limit_bytes=56 * 2**20),
        name="split_rows",
    )(place, own.reshape(shape), got.reshape(shape))


def joined(x_keep, x_got, x_last, y_keep, y_got, y_last, axis):
    return jnp.concatenate(
        [
            x_keep[0].astype(f32) + x_got[0].astype(f32) + x_last.astype(f32),
            y_keep[0].astype(f32) + y_got[1].astype(f32) + y_last.astype(f32),
        ],
        axis=axis,
    ).astype(bf16)


def window_mask(info, dims, micro, piece):
    sub, window, keys, pad, seqs = dims
    base = piece * window + info[1] * sub
    query = base + lax.broadcasted_iota(jnp.int32, (sub, 1), 0)
    start = jnp.zeros((sub, 1), jnp.int32)
    end = jnp.int32(0)
    for k in range(seqs - 1):
        end = end + info[2 + micro * seqs + k]
        start = jnp.where(query >= end, end, start)
    lowest = jnp.maximum(start, query - (window - 1))
    key = base - pad + lax.broadcasted_iota(jnp.int32, (sub, keys), 1)
    return jnp.where((key >= lowest) & (key <= query), 0.0, masked_out).astype(f32)


def fill_window(info, dims, micro_count, pieces, blocks, key_all, value_all):
    sub, window, keys, pad, seqs = dims
    head_size = key_all.shape[-1]
    key_all[:, :pad, :] = jnp.zeros((micro_count, pad, head_size), bf16)
    value_all[:, :pad, :] = jnp.zeros((micro_count, pad, head_size), bf16)
    slots = micro_count * pieces
    offset = {0: 0, 1: 0, 2: 0, 3: 0}
    for mask, block in zip((0, 1, 2, 3, 3), blocks):
        member = info[0] ^ mask
        first = offset[mask]
        amount = block.shape[0] // sub

        def copy(step, carry, block=block, member=member, first=first):
            index = step + first
            row = pl.multiple_of(
                pad + (index % pieces) * window + ((index // slots) * plane + member) * sub, 16
            )
            micro = (index // pieces) % micro_count
            rows = block[pl.ds(pl.multiple_of(step * sub, 16), sub), :]
            key_all[micro, pl.ds(row, sub), :] = rows[:, :head_size]
            value_all[micro, pl.ds(row, sub), :] = rows[:, head_size:]
            return carry

        lax.fori_loop(0, amount, copy, 0)
        offset[mask] = first + amount


def stack_heads(ref, rows, heads, head_size):
    block = ref[rows, :]
    return jnp.concatenate(
        [block[:, h * head_size : (h + 1) * head_size] for h in heads], axis=0
    )


def attend_forward_kernel(
    dims, micro_count, pieces, group, info, q_ref, k0, k1, k2, k3, k4, o_ref, lse_ref, key_all, value_all
):
    sub, window, keys, pad, seqs = dims
    head_size = key_all.shape[-1]
    head_count = q_ref.shape[1] // head_size
    fill_window(info, dims, micro_count, pieces, (k0, k1, k2, k3, k4), key_all, value_all)
    scale = 1.0 / math.sqrt(head_size) / math.log(2.0)

    def slot(index, carry):
        micro = index // pieces
        piece = index % pieces
        bias = window_mask(info, dims, micro, piece)
        start = pl.multiple_of(piece * window + info[1] * sub, 16)
        key_part = key_all[micro, pl.ds(start, keys), :]
        value_part = value_all[micro, pl.ds(start, keys), :]
        rows = pl.ds(pl.multiple_of(index * sub, 16), sub)
        for first in range(0, head_count, group):
            heads = range(first, first + group)
            queries = stack_heads(q_ref, rows, heads, head_size)
            scores = product_nt(queries, key_part) * scale
            scores = scores.reshape(group, sub, keys) + bias[None]
            scores = scores.reshape(group * sub, keys)
            top = jnp.max(scores, axis=-1, keepdims=True)
            weights = jnp.exp2(scores - top)
            total = jnp.sum(weights, axis=-1, keepdims=True)
            mixed = (product(weights.astype(bf16), value_part) / total).astype(bf16)
            for at, h in enumerate(heads):
                o_ref[rows, h * head_size : (h + 1) * head_size] = mixed[at * sub : (at + 1) * sub]
            lse_ref[index, first * sub : (first + group) * sub, :] = top + jnp.log2(total)
        return carry

    lax.fori_loop(0, micro_count * pieces, slot, 0)


def attend_backward_kernel(
    dims,
    micro_count,
    pieces,
    group,
    info,
    q_ref,
    g_ref,
    lse_ref,
    k0,
    k1,
    k2,
    k3,
    k4,
    dq_ref,
    kx_send,
    kx_keep,
    vy_send,
    vy_keep,
    key_all,
    value_all,
    dkey_all,
    dvalue_all,
):
    sub, window, keys, pad, seqs = dims
    head_size = key_all.shape[-1]
    head_count = q_ref.shape[1] // head_size
    fill_window(info, dims, micro_count, pieces, (k0, k1, k2, k3, k4), key_all, value_all)
    dkey_all[...] = jnp.zeros(dkey_all.shape, f32)
    dvalue_all[...] = jnp.zeros(dvalue_all.shape, f32)
    plain = 1.0 / math.sqrt(head_size)
    scale = plain / math.log(2.0)

    def slot(index, carry):
        micro = index // pieces
        piece = index % pieces
        bias = window_mask(info, dims, micro, piece)
        start = pl.multiple_of(piece * window + info[1] * sub, 16)
        key_part = key_all[micro, pl.ds(start, keys), :]
        value_part = value_all[micro, pl.ds(start, keys), :]
        rows = pl.ds(pl.multiple_of(index * sub, 16), sub)
        dkey = jnp.zeros((keys, head_size), f32)
        dvalue = jnp.zeros((keys, head_size), f32)
        for first in range(0, head_count, group):
            heads = range(first, first + group)
            queries = stack_heads(q_ref, rows, heads, head_size)
            grads = stack_heads(g_ref, rows, heads, head_size)
            lse = lse_ref[index, first * sub : (first + group) * sub, :]
            scores = product_nt(queries, key_part) * scale
            scores = scores.reshape(group, sub, keys) + bias[None]
            prob = jnp.exp2(scores.reshape(group * sub, keys) - lse)
            dprob = product_nt(grads, value_part)
            delta = jnp.sum(prob * dprob, axis=-1, keepdims=True)
            dscore = (prob * (dprob - delta)).astype(bf16)
            dquery = (product(dscore, key_part) * plain).astype(bf16)
            for at, h in enumerate(heads):
                dq_ref[rows, h * head_size : (h + 1) * head_size] = dquery[
                    at * sub : (at + 1) * sub
                ]
            dkey = dkey + product_tn(dscore, queries)
            dvalue = dvalue + product_tn(prob.astype(bf16), grads)
        dkey_all[micro, pl.ds(start, keys), :] += dkey * plain
        dvalue_all[micro, pl.ds(start, keys), :] += dvalue
        return carry

    lax.fori_loop(0, micro_count * pieces, slot, 0)
    slots = micro_count * pieces
    for mask, k_out, k_at, v_out, v_at in (
        (0, kx_keep, 0, vy_keep, 0),
        (1, kx_send, 0, vy_keep, 1),
        (2, kx_keep, 1, vy_send, 1),
        (3, kx_send, 1, vy_send, 0),
    ):
        member = info[0] ^ mask

        def copy(index, carry, member=member, k_out=k_out, k_at=k_at, v_out=v_out, v_at=v_at):
            row = pl.multiple_of(
                pad + (index % pieces) * window + ((index // slots) * plane + member) * sub, 16
            )
            micro = (index // pieces) % micro_count
            to = pl.ds(pl.multiple_of(index * sub, 16), sub)
            k_out[k_at, to, :] = dkey_all[micro, pl.ds(row, sub), :].astype(bf16)
            v_out[v_at, to, :] = dvalue_all[micro, pl.ds(row, sub), :].astype(bf16)
            return carry

        lax.fori_loop(0, kx_keep.shape[1] // sub, copy, 0)


def attention_calls(micro_count, pieces, sub, window, head_size, head_count, seqs, kv_rows):
    keys = -(-(window + sub) // 128) * 128
    pad = keys - sub
    dims = (sub, window, keys, pad, seqs)
    group = max(g for g in range(1, head_count + 1) if head_count % g == 0 and g * sub <= max(384, sub))
    token_count = micro_count * pieces * sub
    width = head_count * head_size
    smem = pl.BlockSpec(memory_space=pltpu.SMEM)
    vmem = pl.BlockSpec(memory_space=pltpu.VMEM)
    shape = jax.ShapeDtypeStruct
    span = pad + pieces * window
    work = token_count * head_count * keys
    lse_shape = shape((micro_count * pieces, head_count * sub, 1), f32)
    params = pltpu.CompilerParams(vmem_limit_bytes=56 * 2**20)
    forward = pl.pallas_call(
        functools.partial(attend_forward_kernel, dims, micro_count, pieces, group),
        out_shape=(shape((token_count, width), bf16), lse_shape),
        in_specs=[smem] + [vmem] * 6,
        out_specs=(vmem, vmem),
        scratch_shapes=[pltpu.VMEM((micro_count, span, head_size), bf16)] * 2,
        cost_estimate=pl.CostEstimate(
            flops=4 * work * head_size, transcendentals=work, bytes_accessed=4 * 2**20
        ),
        compiler_params=params,
        name="attend_forward",
    )
    block = shape((2, kv_rows, head_size), bf16)
    backward = pl.pallas_call(
        functools.partial(attend_backward_kernel, dims, micro_count, pieces, group),
        out_shape=(shape((token_count, width), bf16), block, block, block, block),
        in_specs=[smem] + [vmem] * 8,
        out_specs=(vmem,) * 5,
        scratch_shapes=[pltpu.VMEM((micro_count, span, head_size), bf16)] * 2
        + [pltpu.VMEM((micro_count, span, head_size), f32)] * 2,
        cost_estimate=pl.CostEstimate(
            flops=10 * work * head_size, transcendentals=work, bytes_accessed=8 * 2**20
        ),
        compiler_params=params,
        name="attend_backward",
    )
    return forward, backward


def outproj_kernel(core, att, own, other, tokens, gain, residual, normed):
    half = own.shape[1]
    columns = (pl.ds(pl.multiple_of(core[0] * half, 128), half), pl.ds(pl.multiple_of((1 - core[0]) * half, 128), half))
    rows = att[...]
    for weight, cols in zip((own, other), columns):
        residual[:, cols] = product(rows, weight[...])
    total = residual[...] + tokens[...].astype(f32)
    residual[...] = total
    normed[...] = (total * rms_factor(total) * gain[...]).astype(bf16)


def outproj_norm(core, attended, own, other, tokens, gain):
    rows, width = tokens.shape
    vmem = pl.BlockSpec(memory_space=pltpu.VMEM)
    shape = jax.ShapeDtypeStruct
    return pl.pallas_call(
        outproj_kernel,
        out_shape=(shape((rows, width), f32), shape((rows, width), bf16)),
        in_specs=[pl.BlockSpec(memory_space=pltpu.SMEM)] + [vmem] * 5,
        out_specs=(vmem, vmem),
        cost_estimate=pl.CostEstimate(
            flops=2 * rows * width * attended.shape[1],
            transcendentals=0,
            bytes_accessed=2 * width * attended.shape[1] + 10 * rows * width,
        ),
        compiler_params=pltpu.CompilerParams(vmem_limit_bytes=56 * 2**20),
        name="outproj_norm",
    )(core, attended, own, other, tokens, gain)


def feed_kernel(
    core, h0, h1, h2, h3, h4, c0, c1, c2, c3, c4, w_own, w_other, d_own, d_other,
    h_all, c_all, hidden, g_own, g_other, x_send, x_keep, y_send, y_keep, total,
):
    rows = h0.shape[0]
    cut = rows // 2
    for out, blocks in ((h_all, (h0, h1, h3, h4, h2)), (c_all, (c0, c1, c3, c4, c2))):
        at = 0
        for block in blocks:
            out[at : at + block.shape[0], :] = block[...]
            at += block.shape[0]
    half = d_own.shape[1]
    part = hidden.shape[1]
    step = 384 if part % 384 == 0 else part
    is_first = core[0] == 0
    mine = pl.ds(pl.multiple_of(core[0] * half, 128), half)
    theirs = pl.ds(pl.multiple_of((1 - core[0]) * half, 128), half)
    root = math.sqrt(2.0 / math.pi)

    def block(index, carry):
        at = pl.ds(pl.multiple_of(index * rows, 16), rows)
        tokens = h_all[at, :]
        up_mine = c_all[at, mine]
        up_theirs = c_all[at, theirs]
        for first in range(0, part, step):
            cols = slice(first, first + step)
            pre_own = product(tokens, w_own[:, cols])
            pre_other = product(tokens, w_other[:, cols])
            gate = jnp.where(is_first, pre_own, pre_other)
            upward = jnp.where(is_first, pre_other, pre_own)
            grad = product_nt(up_mine, d_own[cols, :]) + product_nt(up_theirs, d_other[cols, :])
            square = gate * gate
            curve = jnp.tanh(root * gate * (1.0 + 0.044715 * square))
            lift = 0.5 * (1.0 + curve)
            active = gate * lift
            slope = lift + (0.5 * root) * gate * (1.0 - curve * curve) * (
                1.0 + (3 * 0.044715) * square
            )
            hidden[at, cols] = (active * upward).astype(bf16)
            grad_gate = grad * upward * slope
            grad_up = grad * active
            mine_in = jnp.where(is_first, grad_gate, grad_up).astype(bf16)
            theirs_in = jnp.where(is_first, grad_up, grad_gate).astype(bf16)
            g_own[at, cols] = mine_in
            g_other[at, cols] = theirs_in
            back = product_nt(mine_in, w_own[:, cols]) + product_nt(theirs_in, w_other[:, cols])
            if first == 0:
                total[at, :] = back
            else:
                total[at, :] += back
        return carry

    lax.fori_loop(0, plane, block, 0)
    width = total.shape[1] // 2
    for out, slot, member in (
        (x_keep, 0, 0), (x_send, 0, 1), (x_send, 1, 2), (x_keep, 1, 3),
    ):
        out[slot] = total[member * rows : (member + 1) * rows, :width].astype(bf16)
    for out, slot, member in (
        (y_keep, 0, 0), (y_keep, 1, 1), (y_send, 0, 2), (y_send, 1, 3),
    ):
        out[slot] = total[member * rows : (member + 1) * rows, width:].astype(bf16)


def feed_forward(core, h_blocks, c_blocks, w_own, w_other, d_own, d_other):
    rows, width = h_blocks[0].shape
    part = w_own.shape[1]
    count = plane * rows
    vmem = pl.BlockSpec(memory_space=pltpu.VMEM)
    shape = jax.ShapeDtypeStruct
    wide = shape((count, part), bf16)
    sent = shape((2, rows, width // 2), bf16)
    return pl.pallas_call(
        feed_kernel,
        out_shape=(shape((count, width), bf16),) * 2 + (wide,) * 3 + (sent,) * 4,
        in_specs=[pl.BlockSpec(memory_space=pltpu.SMEM)] + [vmem] * 14,
        out_specs=(vmem,) * 9,
        scratch_shapes=[pltpu.VMEM((count, width), f32)],
        cost_estimate=pl.CostEstimate(
            flops=10 * count * width * part,
            transcendentals=count * part,
            bytes_accessed=8 * width * part + 12 * count * part,
        ),
        compiler_params=pltpu.CompilerParams(vmem_limit_bytes=58 * 2**20),
        name="feed_forward",
    )(core, *h_blocks, *c_blocks, w_own, w_other, d_own, d_other)


def norm_two_kernel(
    core, x_keep, x_got, x_last, y_keep, y_got, y_last, residual, up, gain, own, other,
    grad_out, attn, mixed, grad_gain,
):
    width = x_last.shape[1]
    half = own.shape[1]
    mine = pl.ds(pl.multiple_of(core[0] * half, 128), half)
    theirs = pl.ds(pl.multiple_of((1 - core[0]) * half, 128), half)
    upstream = jnp.concatenate(
        [
            x_keep[0].astype(f32) + x_got[0].astype(f32) + x_last[...].astype(f32),
            y_keep[0].astype(f32) + y_got[1].astype(f32) + y_last[...].astype(f32),
        ],
        axis=1,
    )
    values = residual[...]
    factor = rms_factor(values)
    grad_gain[...] = jnp.sum(upstream * values * factor, axis=0, keepdims=True)
    total = up[...].astype(f32) + norm_backward(values, factor, gain[...], upstream)
    grad_out[...] = total
    attn[...] = total.astype(bf16)
    mixed[...] = (
        product_nt(attn[:, mine], own[...]) + product_nt(attn[:, theirs], other[...])
    ).astype(bf16)


def norm_two_backward(core, sums, residual, up, gain, own, other):
    rows, width = residual.shape
    vmem = pl.BlockSpec(memory_space=pltpu.VMEM)
    shape = jax.ShapeDtypeStruct
    return pl.pallas_call(
        norm_two_kernel,
        out_shape=(
            shape((rows, width), f32),
            shape((rows, width), bf16),
            shape((rows, own.shape[0]), bf16),
            shape((1, width), f32),
        ),
        in_specs=[pl.BlockSpec(memory_space=pltpu.SMEM)] + [vmem] * 11,
        out_specs=(vmem,) * 4,
        cost_estimate=pl.CostEstimate(
            flops=2 * rows * width * own.shape[0],
            transcendentals=0,
            bytes_accessed=2 * width * own.shape[0] + 20 * rows * width,
        ),
        compiler_params=pltpu.CompilerParams(vmem_limit_bytes=56 * 2**20),
        name="norm_two_backward",
    )(core, *sums, residual, up, gain, own, other)


def input_kernel(
    core, partial, dkv, kv_own, kv_other, normed, tokens, gain, other_gain, grad_resid,
    grad_input, last_own, last_other,
):
    head = kv_own.shape[1]
    mine = pl.ds(pl.multiple_of(core[0] * head, 128), head)
    theirs = pl.ds(pl.multiple_of((1 - core[0]) * head, 128), head)
    is_first = core[0] == 0
    upstream = (
        partial[...]
        + product_nt(dkv[:, mine], kv_own[...])
        + product_nt(dkv[:, theirs], kv_other[...])
    )
    values = tokens[...].astype(f32)
    factor = rms_factor(values)
    grad_gain = jnp.sum(upstream * values * factor, axis=0, keepdims=True)
    grad_input[...] = (
        grad_resid[...] + norm_backward(values, factor, gain[...], upstream)
    ).astype(bf16)
    kept = jnp.where(is_first, grad_gain, other_gain[...])
    given = jnp.where(is_first, other_gain[...], grad_gain)
    width = kept.shape[1]
    for out, cols, row in ((last_own, mine, kept), (last_other, theirs, given)):
        out[:, :head] = product_tn(normed[...], dkv[:, cols]).astype(bf16)
        out[:, head:] = jnp.broadcast_to(row, (128, width)).T.astype(bf16)


def input_backward(core, partial, dkv, kv_own, kv_other, normed, tokens, gain, other_gain, grad_resid):
    rows, width = tokens.shape
    vmem = pl.BlockSpec(memory_space=pltpu.VMEM)
    shape = jax.ShapeDtypeStruct
    last = shape((width, kv_own.shape[1] + 128), bf16)
    return pl.pallas_call(
        input_kernel,
        out_shape=(shape((rows, width), bf16), last, last),
        in_specs=[pl.BlockSpec(memory_space=pltpu.SMEM)] + [vmem] * 9,
        out_specs=(vmem,) * 3,
        cost_estimate=pl.CostEstimate(
            flops=8 * rows * width * kv_own.shape[1],
            transcendentals=0,
            bytes_accessed=16 * rows * width,
        ),
        compiler_params=pltpu.CompilerParams(vmem_limit_bytes=56 * 2**20),
        name="input_backward",
    )(core, partial, dkv, kv_own, kv_other, normed, tokens, gain, other_gain, grad_resid)


def on_device(
    tokens,
    lengths,
    piece_order,
    predecessor,
    gain_one,
    query_weight,
    keyval_weight,
    outproj_weight,
    gain_two,
    gate_weight,
    up_weight,
    down_weight,
    cotangent,
):
    shard_count = lax.axis_size("shard")
    grp_count = lax.axis_size("grp")
    lead = shard_count // plane
    micro_count, piece_count, sub_rows, feat = tokens.shape
    window = sub_rows * shard_count
    token_count = micro_count * piece_count * sub_rows
    head_size = keyval_weight.shape[1] // 2
    width = query_weight.shape[1]
    head_count = width // head_size
    hidden_width = gate_weight.shape[1]
    my_rows = query_weight.shape[0]
    my_hidden = down_weight.shape[0]
    part = hidden_width // plane
    half_w = width // 2
    half_d = feat // 2
    my_index = lax.axis_index("shard")
    my_place = my_index % plane
    core = lax.axis_index("grp") % 2
    first_core = core == 0

    def in_order(own, other):
        return jnp.where(
            first_core,
            jnp.concatenate([own, other], axis=1),
            jnp.concatenate([other, own], axis=1),
        )

    def halves(value):
        size = value.shape[1] // 2
        return (
            lax.dynamic_slice_in_dim(value, core * size, size, 1),
            lax.dynamic_slice_in_dim(value, (1 - core) * size, size, 1),
        )

    place = jnp.stack([my_place, my_index]).astype(jnp.int32)

    def by_lead(value):
        return value.reshape(lead, my_rows, -1)

    def plane_weight(blocks):
        return place_plane(blocks, place).reshape(feat, -1)

    qo_line = gather_column(
        jnp.concatenate([halves(query_weight)[0], halves(outproj_weight)[0]], axis=1)
    )
    gain_cols = jnp.pad(jnp.stack([gain_one, gain_two], axis=1), ((0, 0), (0, 126)))
    kv_mine = jnp.concatenate([halves(keyval_weight)[0], gain_cols], axis=1)
    kv_line = gather_column(kv_mine)
    upstream = cotangent.reshape(token_count, feat)
    gate_or_up = jnp.where(first_core, gate_weight, up_weight)
    up_first, up_second, kv_line, gate_or_up = tie(
        *start_plane(upstream), by_lead(kv_line), gate_or_up
    )
    pieces_out = jnp.transpose(
        gate_or_up.reshape(my_rows, lead, plane, my_hidden), (2, 0, 1, 3)
    ).reshape(plane, my_rows, part)
    wide_in = jnp.zeros((plane, my_rows, part), bf16)
    for mask in range(plane):
        block = lax.dynamic_index_in_dim(pieces_out, my_place ^ mask, axis=0, keepdims=True)
        block = block if mask == 0 else across(block, mask)
        wide_in = lax.dynamic_update_slice_in_dim(wide_in, block, my_place ^ mask, axis=0)
    kv_own = plane_weight(gather_plane(kv_line))
    kv_own, qo_line = tie(kv_own, qo_line)
    query_line, out_line = by_lead(qo_line[:, :half_w]), by_lead(qo_line[:, half_w:])
    query_first, query_second = start_plane(query_line)
    out_first, out_second = start_plane(out_line)
    kv_other = peer(kv_own)
    gains = kv_own[:, head_size : head_size + 2].T
    kv_own, kv_other = kv_own[:, :head_size], kv_other[:, :head_size]
    full_gain_one = gains[0].astype(f32)
    full_gain_two = gains[1].astype(f32)

    stream = tokens.reshape(token_count, feat).astype(f32)
    factor_one = rms_factor(stream)
    normed_one = (stream * factor_one * full_gain_one).astype(bf16)
    keyvals = in_order(product(normed_one, kv_own), product(normed_one, kv_other)).astype(bf16)
    keyvals, wide_in = tie(keyvals, wide_in)
    wide_own = gather_column(wide_in.reshape(plane * my_rows, part))
    down_own = gather_column(halves(down_weight)[0])
    keyvals_line, query_first, query_second, out_first, out_second = tie(
        gather_column(keyvals), query_first, query_second, out_first, out_second
    )
    query_blocks = finish_plane(query_line, query_first, query_second)
    key_first, key_second, *query_blocks = tie(*start_plane(keyvals_line), *query_blocks)
    query_own = plane_weight(query_blocks)
    kv_blocks = finish_plane(keyvals_line, key_first, key_second)
    out_blocks = finish_plane(out_line, out_first, out_second)
    *blocks, query_own = tie(*kv_blocks, *out_blocks, query_own)
    kv_blocks, out_blocks = blocks[:5], blocks[5:]
    out_own = plane_weight(out_blocks)
    query_other = peer(query_own)
    out_other = peer(out_own)
    queries = in_order(product(normed_one, query_own), product(normed_one, query_other)).astype(bf16)
    forward, backward = attention_calls(
        micro_count,
        piece_count,
        sub_rows,
        window,
        head_size,
        head_count,
        lengths.shape[-1],
        lead * token_count,
    )
    info = jnp.concatenate([place, lengths.reshape(-1).astype(jnp.int32)])
    attended, logsum = forward(info, queries, *kv_blocks)
    attended, *up_blocks = tie(attended, *finish_plane(upstream, up_first, up_second))
    core_info = core.astype(jnp.int32).reshape(1)
    gain_two_row = full_gain_two.reshape(1, feat)
    residual, normed_two = outproj_norm(
        core_info,
        attended,
        out_own,
        out_other,
        tokens.reshape(token_count, feat),
        gain_two_row,
    )

    normed_first, normed_second, wide_own, down_own = tie(
        *start_plane(normed_two), wide_own, down_own
    )
    normed_blocks = finish_plane(normed_two, normed_first, normed_second)
    wide_other = peer(wide_own)
    down_other = peer(down_own)
    all_normed, all_up, hidden, grad_own_in, grad_other_in, *sums = feed_forward(
        core_info, normed_blocks, up_blocks, wide_own, wide_other, down_own, down_other
    )
    up_own, up_other = halves(all_up)

    def chip_sum(own, other):
        return (own.astype(f32) + peer(other.astype(bf16)).astype(f32)).astype(bf16)

    wide_peer = product_tn(all_normed, grad_other_in).astype(bf16)
    wide_mine = product_tn(all_normed, grad_own_in).astype(bf16)
    out_mine = product(hidden, down_own).astype(bf16)
    out_peer = product(hidden, down_other).astype(bf16)
    x_send, x_keep, y_send, y_keep = sums
    x_got, x_last, y_got, y_last, during_first, during_second = exchange_plane(
        x_send,
        x_keep,
        y_send,
        y_keep,
        (wide_mine, wide_peer),
        (
            out_mine,
            out_peer,
            product_tn(hidden, up_own).astype(bf16),
            product_tn(hidden, up_other).astype(bf16),
        ),
    )
    out_mine, out_peer, *down_parts = during_second
    wide_grad = scatter_column(chip_sum(*during_first))
    down_grad = scatter_column(chip_sum(*down_parts))
    grad_resid, grad_attn, grad_mixed, grad_gain_two = norm_two_backward(
        core_info,
        (x_keep, x_got, x_last, y_keep, y_got, y_last),
        residual,
        upstream,
        gain_two_row,
        out_own,
        out_other,
    )

    one = out_mine.reshape(plane, token_count, -1)
    two = out_peer.reshape(plane, token_count, -1)
    out_parts = (one[1:3], (one[0], one[3]), two[2:4], (two[0], two[1]))
    grad_queries, kx_send, kx_keep, vy_send, vy_keep = backward(
        info, queries, grad_mixed, logsum, *kv_blocks
    )
    out_x, out_x_last, out_y, out_y_last, kernel_out, _ = exchange_plane(
        *out_parts, (grad_queries, kx_send, kx_keep, vy_send, vy_keep, grad_attn)
    )
    grad_queries, kx_send, kx_keep, vy_send, vy_keep, grad_attn = kernel_out
    out_sum = (
        one[0].astype(f32) + out_x[0].astype(f32) + out_x_last.astype(f32),
        two[0].astype(f32) + out_y[1].astype(f32) + out_y_last.astype(f32),
    )
    block_output = (residual + in_order(*out_sum)).astype(bf16).reshape(tokens.shape)

    dq_own, dq_other = halves(grad_queries)
    da_own, da_other = halves(grad_attn)
    attn_mine = product_tn(attended, da_own).astype(bf16)
    attn_peer = peer(product_tn(attended, da_other).astype(bf16))
    kx_got, kx_last, vy_got, vy_last, attn_parts, query_parts = exchange_plane(
        kx_send,
        kx_keep,
        vy_send,
        vy_keep,
        (attn_mine, attn_peer),
        (
            product_tn(normed_one, dq_own).astype(bf16),
            product_tn(normed_one, dq_other).astype(bf16),
        ),
    )
    grad_kv, wide_grad = tie(
        joined(kx_keep, kx_got, kx_last, vy_keep, vy_got, vy_last, 1), wide_grad
    )
    attn_split = split_rows(place, *attn_parts, my_rows)
    query_split = split_rows(place, query_parts[0], peer(query_parts[1]), my_rows)
    partial = product_nt(dq_own, query_own) + product_nt(dq_other, query_other)
    grad_keyvals, (attn_split, query_split) = halve_column(
        grad_kv, my_index // plane, (attn_split, (*query_split, partial))
    )
    *query_split, partial = query_split
    wide_grad = wide_grad.reshape(plane, my_rows, part)

    def plane_rows(x_send, x_keep, y_send, y_keep):
        x_got, x_last, y_got, y_last, _, _ = exchange_plane(x_send, x_keep, y_send, y_keep)
        total = joined(x_keep, x_got, x_last, y_keep, y_got, y_last, 0)
        return total.reshape(lead * my_rows, -1)

    attn_plane = plane_rows(*attn_split)
    query_plane = plane_rows(*query_split)
    input_grad, last_own, last_other = input_backward(
        core_info,
        partial,
        grad_keyvals,
        kv_own,
        kv_other,
        normed_one,
        tokens.reshape(token_count, feat),
        full_gain_one.reshape(1, feat),
        grad_gain_two,
        grad_resid,
    )
    input_grad = input_grad.reshape(tokens.shape)
    last_plane = plane_rows(*split_rows(place, last_own, peer(last_other), my_rows))
    last_plane, down_grad = tie(last_plane, down_grad)
    last_share = scatter_column(
        jnp.concatenate([query_plane, attn_plane, last_plane], axis=1)
    )

    wide_back = []
    for mask in range(plane):
        block = lax.dynamic_index_in_dim(wide_grad, my_place ^ mask, axis=0, keepdims=False)
        wide_back.append(block if mask == 0 else across(block, mask))
    wide_share = unshuffle(wide_back, place, my_hidden)

    def whole(share):
        total = share
        for step in range(1, grp_count // 2):
            moved = lax.ppermute(
                share, "grp", [(i, (i + 2 * step) % grp_count) for i in range(grp_count)]
            )
            total = total.astype(f32) + moved.astype(f32)
        total = total.astype(bf16)
        return total.astype(f32), peer(total).astype(f32)

    wide_one, wide_two = whole(wide_share)
    down_pair = whole(down_grad)
    last_pair = whole(last_share)
    query_pair = [share[:, :half_w] for share in last_pair]
    out_pair = [share[:, half_w : half_w + half_d] for share in last_pair]
    last_one, last_two = [share[:, half_w + half_d :] for share in last_pair]
    return (
        block_output,
        input_grad,
        jnp.where(first_core, last_one[:, head_size], last_two[:, head_size]),
        in_order(*query_pair),
        in_order(last_one[:, :head_size], last_two[:, :head_size]),
        in_order(*out_pair),
        jnp.where(first_core, last_two[:, head_size], last_one[:, head_size]),
        jnp.where(first_core, wide_one, wide_two),
        jnp.where(first_core, wide_two, wide_one),
        in_order(*down_pair),
    )


def solution(mesh):
    in_specs = (
        P(None, "grp", "shard", None),
        P(None, "grp", None),
        P(None, "grp", None),
        P(None, "grp", None),
        P("shard"),
        P("shard", None),
        P("shard", None),
        P("shard", None),
        P("shard"),
        P("shard", None),
        P("shard", None),
        P("shard", None),
        P(None, "grp", "shard", None),
    )
    out_specs = (
        P(None, "grp", "shard", None),
        P(None, "grp", "shard", None),
        P("shard"),
        P("shard", None),
        P("shard", None),
        P("shard", None),
        P("shard"),
        P("shard", None),
        P("shard", None),
        P("shard", None),
    )
    return jax.shard_map(
        on_device, mesh=mesh, in_specs=in_specs, out_specs=out_specs, check_vma=False
    )
```

```python
import functools
import math

import jax
import jax.numpy as jnp
from jax import lax
from jax.experimental import pallas as pl
from jax.experimental.pallas import tpu as pltpu
from jax.sharding import PartitionSpec as P

epsilon = 1e-06
masked_out = -1e30
bf16 = jnp.bfloat16
f32 = jnp.float32
plane = 4
ring_order = (0, 1, 3, 2)


def rms_factor(values):
    return lax.rsqrt(jnp.mean(values * values, axis=-1, keepdims=True) + epsilon)


def product(first_op, second_op):
    return jnp.dot(first_op, second_op, preferred_element_type=f32)


def product_tn(first_op, second_op):
    return lax.dot_general(
        first_op, second_op, (((0,), (0,)), ((), ())), preferred_element_type=f32
    )


def product_nt(first_op, second_op):
    return lax.dot_general(
        first_op, second_op, (((1,), (1,)), ((), ())), preferred_element_type=f32
    )


def norm_backward(values, factor, gain, upstream):
    inner_mean = jnp.mean(gain * upstream * values, axis=-1, keepdims=True)
    return factor * gain * upstream - values * factor * factor * factor * inner_mean


def tie(*values):
    return lax.optimization_barrier(values)


def across(value, mask):
    count = lax.axis_size("shard")
    return lax.ppermute(value, "shard", [(i, i ^ mask) for i in range(count)])


def peer(value):
    count = lax.axis_size("grp")
    return lax.ppermute(value, "grp", [(i, i ^ 1) for i in range(count)])


def column_groups():
    count = lax.axis_size("shard")
    return [[a * plane + b for a in range(count // plane)] for b in range(plane)]


def gather_column(value):
    return lax.all_gather(
        value, "shard", axis=0, tiled=True, axis_index_groups=column_groups()
    )


def scatter_column(value):
    return lax.psum_scatter(
        value, "shard", scatter_dimension=0, tiled=True, axis_index_groups=column_groups()
    )


def double_column(value):
    held = value[None]
    while held.shape[0] < lax.axis_size("shard") // plane:
        got = across(held, held.shape[0] * plane)
        held = jnp.concatenate([held, got], axis=0)
    return held


def halve_column(held, *during):
    during = list(during)
    ready = ()
    while held.shape[0] > 1:
        size = held.shape[0] // 2
        got = across(held[size:], size * plane)
        if during:
            got, *ready = tie(got, *during.pop(0)(*ready))
        held = (held[:size].astype(f32) + got.astype(f32)).astype(bf16)
    for rest in during:
        ready = rest(*ready)
    return held[0], ready


def start_plane(value):
    return across(value, 1), across(value, 2)


def finish_plane(value, first, second):
    half = value.shape[0] // 2
    far_top = across(first[:half], 2)
    far_bottom = across(second[half:], 1)
    return value, first, second, far_top, far_bottom


def gather_plane(value):
    return finish_plane(value, *tie(*start_plane(value)))


def place_kernel(relative, place, own, first, second, far_top, far_bottom, out):
    half = far_top.shape[0]
    me = place[0]
    line = place[1] // plane if relative else 0
    for at in range(own.shape[0]):
        far = far_top[at : at + 1] if at < half else far_bottom[at - half : at - half + 1]
        blocks = (own[at : at + 1], first[at : at + 1], second[at : at + 1], far)
        for mask, block in enumerate(blocks):
            out[pl.ds(line ^ at, 1), pl.ds(me ^ mask, 1)] = block[:, None]


def place_plane(blocks, place, relative=False):
    lead, rows, width = blocks[0].shape
    vmem = pl.BlockSpec(memory_space=pltpu.VMEM)
    return pl.pallas_call(
        functools.partial(place_kernel, relative),
        out_shape=jax.ShapeDtypeStruct((lead, plane, rows, width), blocks[0].dtype),
        in_specs=[pl.BlockSpec(memory_space=pltpu.SMEM)] + [vmem] * 5,
        out_specs=vmem,
        cost_estimate=pl.CostEstimate(
            flops=0, transcendentals=0, bytes_accessed=4 * plane * lead * rows * width
        ),
        name="place_plane",
    )(place, *blocks)


def unshuffle(pieces, place, unit):
    rows, part = pieces[0].shape
    lead = part // unit
    vmem = pl.BlockSpec(memory_space=pltpu.VMEM)

    def kernel(place, p0, p1, p2, p3, out, natural):
        for mask, piece in enumerate((p0, p1, p2, p3)):
            natural[pl.ds(place[0] ^ mask, 1)] = piece[...].astype(f32)[None]
        columns = [
            natural[member][:, a * unit : (a + 1) * unit]
            for a in range(lead)
            for member in range(plane)
        ]
        out[...] = jnp.concatenate(columns, axis=1).astype(bf16)

    return pl.pallas_call(
        kernel,
        out_shape=jax.ShapeDtypeStruct((rows, plane * part), bf16),
        in_specs=[pl.BlockSpec(memory_space=pltpu.SMEM)] + [vmem] * 4,
        out_specs=vmem,
        scratch_shapes=[pltpu.VMEM((plane, rows, part), f32)],
        cost_estimate=pl.CostEstimate(
            flops=0, transcendentals=0, bytes_accessed=4 * plane * rows * part
        ),
        name="unshuffle",
    )(place, *pieces)


def pass_plane(x_keep, x_got, y_keep, y_got):
    x_pass, y_pass = tie(
        (x_keep[1].astype(f32) + x_got[1].astype(f32)).astype(bf16),
        (y_keep[1].astype(f32) + y_got[0].astype(f32)).astype(bf16),
    )
    return across(x_pass, 2), across(y_pass, 1)


def exchange_plane(x_send, x_keep, y_send, y_keep, during_first=(), during_second=()):
    x_got, y_got, *during_first = tie(across(x_send, 1), across(y_send, 2), *during_first)
    x_last, y_last = pass_plane(x_keep, x_got, y_keep, y_got)
    x_last, y_last, *during_second = tie(x_last, y_last, *during_second)
    return x_got, x_last, y_got, y_last, during_first, during_second


def split_kernel(place, *refs):
    *pairs, x_send, x_keep, y_send, y_keep = refs
    half = x_send.shape[1]
    for out, slot, mask, first in (
        (x_send, 0, 1, 0),
        (x_send, 1, 3, 0),
        (x_keep, 0, 0, 0),
        (x_keep, 1, 2, 0),
        (y_send, 0, 3, half),
        (y_send, 1, 2, half),
        (y_keep, 0, 0, half),
        (y_keep, 1, 1, half),
    ):
        at = (slice(first, first + half), pl.ds(place[0] ^ mask, 1))
        start = 0
        for own, got in zip(pairs[::2], pairs[1::2]):
            end = start + own.shape[3]
            total = (own[at].astype(f32) + got[at].astype(f32))[:, 0].astype(bf16)
            out[slot, :, :, start:end] = total
            start = end


def split_rows(place, rows, *pairs):
    lead = pairs[0].shape[0] // (plane * rows)
    width = sum(value.shape[1] for value in pairs) // 2
    vmem = pl.BlockSpec(memory_space=pltpu.VMEM)
    sent = jax.ShapeDtypeStruct((2, lead // 2, rows, width), bf16)
    size = width * pairs[0].shape[0]
    return pl.pallas_call(
        split_kernel,
        out_shape=(sent,) * 4,
        in_specs=[pl.BlockSpec(memory_space=pltpu.SMEM)] + [vmem] * len(pairs),
        out_specs=(vmem,) * 4,
        cost_estimate=pl.CostEstimate(flops=size, transcendentals=0, bytes_accessed=6 * size),
        compiler_params=pltpu.CompilerParams(vmem_limit_bytes=56 * 2**20),
        name="split_rows",
    )(place, *(value.reshape(lead, plane, rows, value.shape[1]) for value in pairs))


def joined(x_keep, x_got, x_last, y_keep, y_got, y_last, axis):
    return jnp.concatenate(
        [
            x_keep[0].astype(f32) + x_got[0].astype(f32) + x_last.astype(f32),
            y_keep[0].astype(f32) + y_got[1].astype(f32) + y_last.astype(f32),
        ],
        axis=axis,
    ).astype(bf16)


def window_mask(info, dims, micro, piece):
    sub, window, keys, pad, seqs = dims
    base = piece * window + info[1] * sub
    query = base + lax.broadcasted_iota(jnp.int32, (sub, 1), 0)
    start = jnp.zeros((sub, 1), jnp.int32)
    end = jnp.int32(0)
    for k in range(seqs - 1):
        end = end + info[2 + micro * seqs + k]
        start = jnp.where(query >= end, end, start)
    lowest = jnp.maximum(start, query - (window - 1))
    key = base - pad + lax.broadcasted_iota(jnp.int32, (sub, keys), 1)
    return jnp.where((key >= lowest) & (key <= query), 0.0, masked_out).astype(f32)


def fill_window(info, dims, micro_count, pieces, blocks, key_all, value_all):
    sub, window, keys, pad, seqs = dims
    head_size = key_all.shape[-1]
    key_all[:, :pad, :] = jnp.zeros((micro_count, pad, head_size), bf16)
    value_all[:, :pad, :] = jnp.zeros((micro_count, pad, head_size), bf16)
    slots = micro_count * pieces
    offset = {0: 0, 1: 0, 2: 0, 3: 0}
    for mask, block in zip((0, 1, 2, 3, 3), blocks):
        member = info[0] ^ mask
        first = offset[mask]
        amount = block.shape[0] // sub

        def copy(step, carry, block=block, member=member, first=first):
            index = step + first
            row = pl.multiple_of(
                pad + (index % pieces) * window + ((index // slots) * plane + member) * sub, 16
            )
            micro = (index // pieces) % micro_count
            rows = block[pl.ds(pl.multiple_of(step * sub, 16), sub), :]
            key_all[micro, pl.ds(row, sub), :] = rows[:, :head_size]
            value_all[micro, pl.ds(row, sub), :] = rows[:, head_size:]
            return carry

        lax.fori_loop(0, amount, copy, 0)
        offset[mask] = first + amount


def stack_heads(ref, rows, heads, head_size):
    block = ref[rows, :]
    return jnp.concatenate(
        [block[:, h * head_size : (h + 1) * head_size] for h in heads], axis=0
    )


def attend_forward_kernel(
    dims, micro_count, pieces, group, info, q_ref, k0, k1, k2, k3, k4, o_ref, lse_ref, key_all, value_all
):
    sub, window, keys, pad, seqs = dims
    head_size = key_all.shape[-1]
    head_count = q_ref.shape[1] // head_size
    fill_window(info, dims, micro_count, pieces, (k0, k1, k2, k3, k4), key_all, value_all)
    scale = 1.0 / math.sqrt(head_size) / math.log(2.0)

    def slot(index, carry):
        micro = index // pieces
        piece = index % pieces
        bias = window_mask(info, dims, micro, piece)
        start = pl.multiple_of(piece * window + info[1] * sub, 16)
        key_part = key_all[micro, pl.ds(start, keys), :]
        value_part = value_all[micro, pl.ds(start, keys), :]
        rows = pl.ds(pl.multiple_of(index * sub, 16), sub)
        for first in range(0, head_count, group):
            heads = range(first, first + group)
            queries = stack_heads(q_ref, rows, heads, head_size)
            scores = product_nt(queries, key_part) * scale
            scores = scores.reshape(group, sub, keys) + bias[None]
            scores = scores.reshape(group * sub, keys)
            top = jnp.max(scores, axis=-1, keepdims=True)
            weights = jnp.exp2(scores - top)
            total = jnp.sum(weights, axis=-1, keepdims=True)
            mixed = (product(weights.astype(bf16), value_part) / total).astype(bf16)
            for at, h in enumerate(heads):
                o_ref[rows, h * head_size : (h + 1) * head_size] = mixed[at * sub : (at + 1) * sub]
            lse_ref[index, first * sub : (first + group) * sub, :] = top + jnp.log2(total)
        return carry

    lax.fori_loop(0, micro_count * pieces, slot, 0)


def attend_backward_kernel(
    dims,
    micro_count,
    pieces,
    group,
    info,
    q_ref,
    g_ref,
    lse_ref,
    k0,
    k1,
    k2,
    k3,
    k4,
    dq_ref,
    kx_send,
    kx_keep,
    vy_send,
    vy_keep,
    key_all,
    value_all,
    dkey_all,
    dvalue_all,
):
    sub, window, keys, pad, seqs = dims
    head_size = key_all.shape[-1]
    head_count = q_ref.shape[1] // head_size
    fill_window(info, dims, micro_count, pieces, (k0, k1, k2, k3, k4), key_all, value_all)
    dkey_all[...] = jnp.zeros(dkey_all.shape, f32)
    dvalue_all[...] = jnp.zeros(dvalue_all.shape, f32)
    plain = 1.0 / math.sqrt(head_size)
    scale = plain / math.log(2.0)

    def slot(index, carry):
        micro = index // pieces
        piece = index % pieces
        bias = window_mask(info, dims, micro, piece)
        start = pl.multiple_of(piece * window + info[1] * sub, 16)
        key_part = key_all[micro, pl.ds(start, keys), :]
        value_part = value_all[micro, pl.ds(start, keys), :]
        rows = pl.ds(pl.multiple_of(index * sub, 16), sub)
        dkey = jnp.zeros((keys, head_size), f32)
        dvalue = jnp.zeros((keys, head_size), f32)
        for first in range(0, head_count, group):
            heads = range(first, first + group)
            queries = stack_heads(q_ref, rows, heads, head_size)
            grads = stack_heads(g_ref, rows, heads, head_size)
            lse = lse_ref[index, first * sub : (first + group) * sub, :]
            scores = product_nt(queries, key_part) * scale
            scores = scores.reshape(group, sub, keys) + bias[None]
            prob = jnp.exp2(scores.reshape(group * sub, keys) - lse)
            dprob = product_nt(grads, value_part)
            delta = jnp.sum(prob * dprob, axis=-1, keepdims=True)
            dscore = (prob * (dprob - delta)).astype(bf16)
            dquery = (product(dscore, key_part) * plain).astype(bf16)
            for at, h in enumerate(heads):
                dq_ref[rows, h * head_size : (h + 1) * head_size] = dquery[
                    at * sub : (at + 1) * sub
                ]
            dkey = dkey + product_tn(dscore, queries)
            dvalue = dvalue + product_tn(prob.astype(bf16), grads)
        dkey_all[micro, pl.ds(start, keys), :] += dkey * plain
        dvalue_all[micro, pl.ds(start, keys), :] += dvalue
        return carry

    lax.fori_loop(0, micro_count * pieces, slot, 0)
    slots = micro_count * pieces
    line = info[1] // plane
    for mask, k_out, k_at, v_out, v_at in (
        (0, kx_keep, 0, vy_keep, 0),
        (1, kx_send, 0, vy_keep, 1),
        (2, kx_keep, 1, vy_send, 1),
        (3, kx_send, 1, vy_send, 0),
    ):
        member = info[0] ^ mask

        def copy(index, carry, member=member, k_out=k_out, k_at=k_at, v_out=v_out, v_at=v_at):
            row = pl.multiple_of(
                pad + (index % pieces) * window + (((index // slots) ^ line) * plane + member) * sub, 16
            )
            micro = (index // pieces) % micro_count
            to = pl.ds(pl.multiple_of(index * sub, 16), sub)
            k_out[k_at, to, :] = dkey_all[micro, pl.ds(row, sub), :].astype(bf16)
            v_out[v_at, to, :] = dvalue_all[micro, pl.ds(row, sub), :].astype(bf16)
            return carry

        lax.fori_loop(0, kx_keep.shape[1] // sub, copy, 0)


def attention_calls(micro_count, pieces, sub, window, head_size, head_count, seqs, kv_rows):
    keys = -(-(window + sub) // 128) * 128
    pad = keys - sub
    dims = (sub, window, keys, pad, seqs)
    group = max(g for g in range(1, head_count + 1) if head_count % g == 0 and g * sub <= max(384, sub))
    token_count = micro_count * pieces * sub
    width = head_count * head_size
    smem = pl.BlockSpec(memory_space=pltpu.SMEM)
    vmem = pl.BlockSpec(memory_space=pltpu.VMEM)
    shape = jax.ShapeDtypeStruct
    span = pad + pieces * window
    work = token_count * head_count * keys
    lse_shape = shape((micro_count * pieces, head_count * sub, 1), f32)
    params = pltpu.CompilerParams(vmem_limit_bytes=56 * 2**20)
    forward = pl.pallas_call(
        functools.partial(attend_forward_kernel, dims, micro_count, pieces, group),
        out_shape=(shape((token_count, width), bf16), lse_shape),
        in_specs=[smem] + [vmem] * 6,
        out_specs=(vmem, vmem),
        scratch_shapes=[pltpu.VMEM((micro_count, span, head_size), bf16)] * 2,
        cost_estimate=pl.CostEstimate(
            flops=4 * work * head_size, transcendentals=work, bytes_accessed=4 * 2**20
        ),
        compiler_params=params,
        name="attend_forward",
    )
    block = shape((2, kv_rows, head_size), bf16)
    backward = pl.pallas_call(
        functools.partial(attend_backward_kernel, dims, micro_count, pieces, group),
        out_shape=(shape((token_count, width), bf16), block, block, block, block),
        in_specs=[smem] + [vmem] * 8,
        out_specs=(vmem,) * 5,
        scratch_shapes=[pltpu.VMEM((micro_count, span, head_size), bf16)] * 2
        + [pltpu.VMEM((micro_count, span, head_size), f32)] * 2,
        cost_estimate=pl.CostEstimate(
            flops=10 * work * head_size, transcendentals=work, bytes_accessed=8 * 2**20
        ),
        compiler_params=params,
        name="attend_backward",
    )
    return forward, backward


def outproj_kernel(core, att, own, other, tokens, gain, residual, normed):
    half = own.shape[1]
    columns = (pl.ds(pl.multiple_of(core[0] * half, 128), half), pl.ds(pl.multiple_of((1 - core[0]) * half, 128), half))
    rows = att[...]
    for weight, cols in zip((own, other), columns):
        residual[:, cols] = product(rows, weight[...])
    total = residual[...] + tokens[...].astype(f32)
    residual[...] = total
    normed[...] = (total * rms_factor(total) * gain[...]).astype(bf16)


def outproj_norm(core, attended, own, other, tokens, gain):
    rows, width = tokens.shape
    vmem = pl.BlockSpec(memory_space=pltpu.VMEM)
    shape = jax.ShapeDtypeStruct
    return pl.pallas_call(
        outproj_kernel,
        out_shape=(shape((rows, width), f32), shape((rows, width), bf16)),
        in_specs=[pl.BlockSpec(memory_space=pltpu.SMEM)] + [vmem] * 5,
        out_specs=(vmem, vmem),
        cost_estimate=pl.CostEstimate(
            flops=2 * rows * width * attended.shape[1],
            transcendentals=0,
            bytes_accessed=2 * width * attended.shape[1] + 10 * rows * width,
        ),
        compiler_params=pltpu.CompilerParams(vmem_limit_bytes=56 * 2**20),
        name="outproj_norm",
    )(core, attended, own, other, tokens, gain)


def feed_kernel(
    core, h0, h1, h2, h3, h4, c0, c1, c2, c3, c4, w_own, w_other, d_own, d_other,
    h_all, c_all, hidden, g_own, g_other, x_send, x_keep, y_send, y_keep, total,
):
    rows = h0.shape[0]
    cut = rows // 2
    for out, blocks in ((h_all, (h0, h1, h3, h4, h2)), (c_all, (c0, c1, c3, c4, c2))):
        at = 0
        for block in blocks:
            out[at : at + block.shape[0], :] = block[...]
            at += block.shape[0]
    half = d_own.shape[1]
    part = hidden.shape[1]
    step = 384 if part % 384 == 0 else part
    is_first = core[0] == 0
    mine = pl.ds(pl.multiple_of(core[0] * half, 128), half)
    theirs = pl.ds(pl.multiple_of((1 - core[0]) * half, 128), half)
    root = math.sqrt(2.0 / math.pi)

    def block(index, carry):
        at = pl.ds(pl.multiple_of(index * rows, 16), rows)
        tokens = h_all[at, :]
        up_mine = c_all[at, mine]
        up_theirs = c_all[at, theirs]
        for first in range(0, part, step):
            cols = slice(first, first + step)
            pre_own = product(tokens, w_own[:, cols])
            pre_other = product(tokens, w_other[:, cols])
            gate = jnp.where(is_first, pre_own, pre_other)
            upward = jnp.where(is_first, pre_other, pre_own)
            grad = product_nt(up_mine, d_own[cols, :]) + product_nt(up_theirs, d_other[cols, :])
            square = gate * gate
            curve = jnp.tanh(root * gate * (1.0 + 0.044715 * square))
            lift = 0.5 * (1.0 + curve)
            active = gate * lift
            slope = lift + (0.5 * root) * gate * (1.0 - curve * curve) * (
                1.0 + (3 * 0.044715) * square
            )
            hidden[at, cols] = (active * upward).astype(bf16)
            grad_gate = grad * upward * slope
            grad_up = grad * active
            mine_in = jnp.where(is_first, grad_gate, grad_up).astype(bf16)
            theirs_in = jnp.where(is_first, grad_up, grad_gate).astype(bf16)
            g_own[at, cols] = mine_in
            g_other[at, cols] = theirs_in
            back = product_nt(mine_in, w_own[:, cols]) + product_nt(theirs_in, w_other[:, cols])
            if first == 0:
                total[at, :] = back
            else:
                total[at, :] += back
        return carry

    lax.fori_loop(0, plane, block, 0)
    width = total.shape[1] // 2
    for out, slot, member in (
        (x_keep, 0, 0), (x_send, 0, 1), (x_send, 1, 2), (x_keep, 1, 3),
    ):
        out[slot] = total[member * rows : (member + 1) * rows, :width].astype(bf16)
    for out, slot, member in (
        (y_keep, 0, 0), (y_keep, 1, 1), (y_send, 0, 2), (y_send, 1, 3),
    ):
        out[slot] = total[member * rows : (member + 1) * rows, width:].astype(bf16)


def feed_forward(core, h_blocks, c_blocks, w_own, w_other, d_own, d_other):
    rows, width = h_blocks[0].shape
    part = w_own.shape[1]
    count = plane * rows
    vmem = pl.BlockSpec(memory_space=pltpu.VMEM)
    shape = jax.ShapeDtypeStruct
    wide = shape((count, part), bf16)
    sent = shape((2, rows, width // 2), bf16)
    return pl.pallas_call(
        feed_kernel,
        out_shape=(shape((count, width), bf16),) * 2 + (wide,) * 3 + (sent,) * 4,
        in_specs=[pl.BlockSpec(memory_space=pltpu.SMEM)] + [vmem] * 14,
        out_specs=(vmem,) * 9,
        scratch_shapes=[pltpu.VMEM((count, width), f32)],
        cost_estimate=pl.CostEstimate(
            flops=10 * count * width * part,
            transcendentals=count * part,
            bytes_accessed=8 * width * part + 12 * count * part,
        ),
        compiler_params=pltpu.CompilerParams(vmem_limit_bytes=58 * 2**20),
        name="feed_forward",
    )(core, *h_blocks, *c_blocks, w_own, w_other, d_own, d_other)


def norm_two_kernel(
    core, x_keep, x_got, x_last, y_keep, y_got, y_last, residual, up, gain, own, other,
    grad_out, attn, mixed, grad_gain,
):
    width = x_last.shape[1]
    half = own.shape[1]
    mine = pl.ds(pl.multiple_of(core[0] * half, 128), half)
    theirs = pl.ds(pl.multiple_of((1 - core[0]) * half, 128), half)
    upstream = jnp.concatenate(
        [
            x_keep[0].astype(f32) + x_got[0].astype(f32) + x_last[...].astype(f32),
            y_keep[0].astype(f32) + y_got[1].astype(f32) + y_last[...].astype(f32),
        ],
        axis=1,
    )
    values = residual[...]
    factor = rms_factor(values)
    grad_gain[...] = jnp.sum(upstream * values * factor, axis=0, keepdims=True)
    total = up[...].astype(f32) + norm_backward(values, factor, gain[...], upstream)
    grad_out[...] = total
    attn[...] = total.astype(bf16)
    mixed[...] = (
        product_nt(attn[:, mine], own[...]) + product_nt(attn[:, theirs], other[...])
    ).astype(bf16)


def norm_two_backward(core, sums, residual, up, gain, own, other):
    rows, width = residual.shape
    vmem = pl.BlockSpec(memory_space=pltpu.VMEM)
    shape = jax.ShapeDtypeStruct
    return pl.pallas_call(
        norm_two_kernel,
        out_shape=(
            shape((rows, width), f32),
            shape((rows, width), bf16),
            shape((rows, own.shape[0]), bf16),
            shape((1, width), f32),
        ),
        in_specs=[pl.BlockSpec(memory_space=pltpu.SMEM)] + [vmem] * 11,
        out_specs=(vmem,) * 4,
        cost_estimate=pl.CostEstimate(
            flops=2 * rows * width * own.shape[0],
            transcendentals=0,
            bytes_accessed=2 * width * own.shape[0] + 20 * rows * width,
        ),
        compiler_params=pltpu.CompilerParams(vmem_limit_bytes=56 * 2**20),
        name="norm_two_backward",
    )(core, *sums, residual, up, gain, own, other)


def input_kernel(
    core, partial, dkv, kv_own, kv_other, normed, tokens, gain, other_gain, grad_resid,
    grad_input, last_own, last_other,
):
    head = kv_own.shape[1]
    mine = pl.ds(pl.multiple_of(core[0] * head, 128), head)
    theirs = pl.ds(pl.multiple_of((1 - core[0]) * head, 128), head)
    is_first = core[0] == 0
    upstream = (
        partial[...]
        + product_nt(dkv[:, mine], kv_own[...])
        + product_nt(dkv[:, theirs], kv_other[...])
    )
    values = tokens[...].astype(f32)
    factor = rms_factor(values)
    grad_gain = jnp.sum(upstream * values * factor, axis=0, keepdims=True)
    grad_input[...] = (
        grad_resid[...] + norm_backward(values, factor, gain[...], upstream)
    ).astype(bf16)
    kept = jnp.where(is_first, grad_gain, other_gain[...])
    given = jnp.where(is_first, other_gain[...], grad_gain)
    width = kept.shape[1]
    for out, cols, row in ((last_own, mine, kept), (last_other, theirs, given)):
        out[:, :head] = product_tn(normed[...], dkv[:, cols]).astype(bf16)
        out[:, head:] = jnp.broadcast_to(row, (128, width)).T.astype(bf16)


def input_backward(core, partial, dkv, kv_own, kv_other, normed, tokens, gain, other_gain, grad_resid):
    rows, width = tokens.shape
    vmem = pl.BlockSpec(memory_space=pltpu.VMEM)
    shape = jax.ShapeDtypeStruct
    last = shape((width, kv_own.shape[1] + 128), bf16)
    return pl.pallas_call(
        input_kernel,
        out_shape=(shape((rows, width), bf16), last, last),
        in_specs=[pl.BlockSpec(memory_space=pltpu.SMEM)] + [vmem] * 9,
        out_specs=(vmem,) * 3,
        cost_estimate=pl.CostEstimate(
            flops=8 * rows * width * kv_own.shape[1],
            transcendentals=0,
            bytes_accessed=16 * rows * width,
        ),
        compiler_params=pltpu.CompilerParams(vmem_limit_bytes=56 * 2**20),
        name="input_backward",
    )(core, partial, dkv, kv_own, kv_other, normed, tokens, gain, other_gain, grad_resid)


def on_device(
    tokens,
    lengths,
    piece_order,
    predecessor,
    gain_one,
    query_weight,
    keyval_weight,
    outproj_weight,
    gain_two,
    gate_weight,
    up_weight,
    down_weight,
    cotangent,
):
    shard_count = lax.axis_size("shard")
    grp_count = lax.axis_size("grp")
    lead = shard_count // plane
    micro_count, piece_count, sub_rows, feat = tokens.shape
    window = sub_rows * shard_count
    token_count = micro_count * piece_count * sub_rows
    head_size = keyval_weight.shape[1] // 2
    width = query_weight.shape[1]
    head_count = width // head_size
    hidden_width = gate_weight.shape[1]
    my_rows = query_weight.shape[0]
    my_hidden = down_weight.shape[0]
    part = hidden_width // plane
    half_w = width // 2
    half_d = feat // 2
    my_index = lax.axis_index("shard")
    my_place = my_index % plane
    core = lax.axis_index("grp") % 2
    first_core = core == 0

    def in_order(own, other):
        return jnp.where(
            first_core,
            jnp.concatenate([own, other], axis=1),
            jnp.concatenate([other, own], axis=1),
        )

    def halves(value):
        size = value.shape[1] // 2
        return (
            lax.dynamic_slice_in_dim(value, core * size, size, 1),
            lax.dynamic_slice_in_dim(value, (1 - core) * size, size, 1),
        )

    place = jnp.stack([my_place, my_index]).astype(jnp.int32)

    def by_lead(value):
        return value.reshape(lead, my_rows, -1)

    def plane_weight(blocks):
        return place_plane(blocks, place).reshape(feat, -1)

    qo_line = gather_column(
        jnp.concatenate([halves(query_weight)[0], halves(outproj_weight)[0]], axis=1)
    )
    gain_cols = jnp.pad(jnp.stack([gain_one, gain_two], axis=1), ((0, 0), (0, 126)))
    kv_mine = jnp.concatenate([halves(keyval_weight)[0], gain_cols], axis=1)
    kv_line = gather_column(kv_mine)
    upstream = cotangent.reshape(token_count, feat)
    gate_or_up = jnp.where(first_core, gate_weight, up_weight)
    up_first, up_second, kv_line, gate_or_up = tie(
        *start_plane(upstream), by_lead(kv_line), gate_or_up
    )
    pieces_out = jnp.transpose(
        gate_or_up.reshape(my_rows, lead, plane, my_hidden), (2, 0, 1, 3)
    ).reshape(plane, my_rows, part)
    wide_in = jnp.zeros((plane, my_rows, part), bf16)
    for mask in range(plane):
        block = lax.dynamic_index_in_dim(pieces_out, my_place ^ mask, axis=0, keepdims=True)
        block = block if mask == 0 else across(block, mask)
        wide_in = lax.dynamic_update_slice_in_dim(wide_in, block, my_place ^ mask, axis=0)
    kv_own = plane_weight(gather_plane(kv_line))
    kv_own, qo_line = tie(kv_own, qo_line)
    query_line, out_line = by_lead(qo_line[:, :half_w]), by_lead(qo_line[:, half_w:])
    query_first, query_second = start_plane(query_line)
    out_first, out_second = start_plane(out_line)
    kv_other = peer(kv_own)
    gains = kv_own[:, head_size : head_size + 2].T
    kv_own, kv_other = kv_own[:, :head_size], kv_other[:, :head_size]
    full_gain_one = gains[0].astype(f32)
    full_gain_two = gains[1].astype(f32)

    stream = tokens.reshape(token_count, feat).astype(f32)
    factor_one = rms_factor(stream)
    normed_one = (stream * factor_one * full_gain_one).astype(bf16)
    keyvals = in_order(product(normed_one, kv_own), product(normed_one, kv_other)).astype(bf16)
    keyvals, wide_in = tie(keyvals, wide_in)
    wide_own = gather_column(wide_in.reshape(plane * my_rows, part))
    down_own = gather_column(halves(down_weight)[0])
    keyvals_line, query_first, query_second, out_first, out_second = tie(
        gather_column(keyvals), query_first, query_second, out_first, out_second
    )
    query_blocks = finish_plane(query_line, query_first, query_second)
    key_first, key_second, *query_blocks = tie(*start_plane(keyvals_line), *query_blocks)
    query_own = plane_weight(query_blocks)
    kv_blocks = finish_plane(keyvals_line, key_first, key_second)
    out_blocks = finish_plane(out_line, out_first, out_second)
    *blocks, query_own = tie(*kv_blocks, *out_blocks, query_own)
    kv_blocks, out_blocks = blocks[:5], blocks[5:]
    out_own = plane_weight(out_blocks)
    query_other = peer(query_own)
    out_other = peer(out_own)
    queries = in_order(product(normed_one, query_own), product(normed_one, query_other)).astype(bf16)
    forward, backward = attention_calls(
        micro_count,
        piece_count,
        sub_rows,
        window,
        head_size,
        head_count,
        lengths.shape[-1],
        lead * token_count,
    )
    info = jnp.concatenate([place, lengths.reshape(-1).astype(jnp.int32)])
    attended, logsum = forward(info, queries, *kv_blocks)
    attended, *up_blocks = tie(attended, *finish_plane(upstream, up_first, up_second))
    core_info = core.astype(jnp.int32).reshape(1)
    gain_two_row = full_gain_two.reshape(1, feat)
    residual, normed_two = outproj_norm(
        core_info,
        attended,
        out_own,
        out_other,
        tokens.reshape(token_count, feat),
        gain_two_row,
    )

    normed_first, normed_second, wide_own, down_own = tie(
        *start_plane(normed_two), wide_own, down_own
    )
    normed_blocks = finish_plane(normed_two, normed_first, normed_second)
    wide_other = peer(wide_own)
    down_other = peer(down_own)
    all_normed, all_up, hidden, grad_own_in, grad_other_in, *sums = feed_forward(
        core_info, normed_blocks, up_blocks, wide_own, wide_other, down_own, down_other
    )
    up_own, up_other = halves(all_up)

    def chip_sum(own, other):
        return (own.astype(f32) + peer(other.astype(bf16)).astype(f32)).astype(bf16)

    wide_peer = product_tn(all_normed, grad_other_in).astype(bf16)
    wide_mine = product_tn(all_normed, grad_own_in).astype(bf16)
    x_send, x_keep, y_send, y_keep = sums
    x_got, y_got, wide_mine, wide_peer = tie(
        across(x_send, 1), across(y_send, 2), wide_mine, wide_peer
    )
    x_pass, y_pass, wide_mine, wide_peer, hidden = tie(
        (x_keep[1].astype(f32) + x_got[1].astype(f32)).astype(bf16),
        (y_keep[1].astype(f32) + y_got[0].astype(f32)).astype(bf16),
        wide_mine,
        wide_peer,
        hidden,
    )
    x_last, y_last, out_mine, out_peer, wide_sum = tie(
        across(x_pass, 2),
        across(y_pass, 1),
        product(hidden, down_own).astype(bf16),
        product(hidden, down_other).astype(bf16),
        chip_sum(wide_mine, wide_peer),
    )
    wide_grad = scatter_column(wide_sum)
    grad_resid, grad_attn, grad_mixed, grad_gain_two = norm_two_backward(
        core_info,
        (x_keep, x_got, x_last, y_keep, y_got, y_last),
        residual,
        upstream,
        gain_two_row,
        out_own,
        out_other,
    )

    one = out_mine.reshape(plane, token_count, -1)
    two = out_peer.reshape(plane, token_count, -1)
    grad_queries, kx_send, kx_keep, vy_send, vy_keep = backward(
        info, queries, grad_mixed, logsum, *kv_blocks
    )
    out_x, out_y, grad_queries, kx_send, kx_keep, vy_send, vy_keep, grad_attn, hidden = tie(
        across(one[1:3], 1),
        across(two[2:4], 2),
        grad_queries,
        kx_send,
        kx_keep,
        vy_send,
        vy_keep,
        grad_attn,
        hidden,
    )
    out_x_last, out_y_last = pass_plane((one[0], one[3]), out_x, (two[0], two[1]), out_y)
    out_sum = (
        one[0].astype(f32) + out_x[0].astype(f32) + out_x_last.astype(f32),
        two[0].astype(f32) + out_y[1].astype(f32) + out_y_last.astype(f32),
    )
    block_output = (residual + in_order(*out_sum)).astype(bf16).reshape(tokens.shape)

    dq_own, dq_other = halves(grad_queries)
    da_own, da_other = halves(grad_attn)
    attn_mine = product_tn(attended, da_own).astype(bf16)
    attn_peer = peer(product_tn(attended, da_other).astype(bf16))
    kx_got, vy_got, attn_mine, attn_peer, query_mine, query_peer = tie(
        across(kx_send, 1),
        across(vy_send, 2),
        attn_mine,
        attn_peer,
        product_tn(normed_one, dq_own).astype(bf16),
        peer(product_tn(normed_one, dq_other).astype(bf16)),
    )
    kx_last, vy_last = pass_plane(kx_keep, kx_got, vy_keep, vy_got)
    kx_last, vy_last, hidden, attn_x, attn_x_keep, attn_y, attn_y_keep = tie(
        kx_last,
        vy_last,
        hidden,
        *split_rows(place, my_rows, query_mine, query_peer, attn_mine, attn_peer),
    )
    attn_x, attn_y = across(attn_x, 1), across(attn_y, 2)
    grad_kv, wide_grad = tie(
        joined(kx_keep, kx_got, kx_last, vy_keep, vy_got, vy_last, 1), wide_grad
    )
    partial = product_nt(dq_own, query_own) + product_nt(dq_other, query_other)

    def first_step():
        return (
            product_tn(hidden, up_own).astype(bf16),
            product_tn(hidden, up_other).astype(bf16),
        )

    def second_step(down_mine, down_peer):
        return partial, down_mine, down_peer, attn_x, attn_y

    grad_keyvals, (partial, down_mine, down_peer, attn_x, attn_y) = halve_column(
        grad_kv.reshape(lead, token_count, -1), first_step, second_step
    )
    grad_keyvals, down_sum = tie(grad_keyvals, chip_sum(down_mine, down_peer))
    down_grad = scatter_column(down_sum)
    wide_grad = wide_grad.reshape(plane, my_rows, part)
    input_grad, last_own, last_other = input_backward(
        core_info,
        partial,
        grad_keyvals,
        kv_own,
        kv_other,
        normed_one,
        tokens.reshape(token_count, feat),
        full_gain_one.reshape(1, feat),
        grad_gain_two,
        grad_resid,
    )
    input_grad = input_grad.reshape(tokens.shape)
    last_split = split_rows(place, my_rows, last_own, peer(last_other))
    attn_x_last, attn_y_last = pass_plane(attn_x_keep, attn_x, attn_y_keep, attn_y)
    attn_plane = joined(
        attn_x_keep, attn_x, attn_x_last, attn_y_keep, attn_y, attn_y_last, 0
    ).reshape(lead * my_rows, -1)
    last_x, last_x_keep, last_y, last_y_keep = last_split
    last_x, last_x_last, last_y, last_y_last, _, _ = exchange_plane(
        last_x, last_x_keep, last_y, last_y_keep
    )
    last_plane = joined(
        last_x_keep, last_x, last_x_last, last_y_keep, last_y, last_y_last, 0
    ).reshape(lead * my_rows, -1)
    last_plane, down_grad = tie(last_plane, down_grad)
    last_share = scatter_column(
        jnp.concatenate([attn_plane, last_plane], axis=1)
    )

    wide_back = []
    for mask in range(plane):
        block = lax.dynamic_index_in_dim(wide_grad, my_place ^ mask, axis=0, keepdims=False)
        wide_back.append(block if mask == 0 else across(block, mask))
    wide_share = unshuffle(wide_back, place, my_hidden)

    def whole(share):
        total = share
        for step in range(1, grp_count // 2):
            moved = lax.ppermute(
                share, "grp", [(i, (i + 2 * step) % grp_count) for i in range(grp_count)]
            )
            total = total.astype(f32) + moved.astype(f32)
        total = total.astype(bf16)
        return total.astype(f32), peer(total).astype(f32)

    wide_one, wide_two = whole(wide_share)
    down_pair = whole(down_grad)
    last_pair = whole(last_share)
    query_pair = [share[:, :half_w] for share in last_pair]
    out_pair = [share[:, half_w : half_w + half_d] for share in last_pair]
    last_one, last_two = [share[:, half_w + half_d :] for share in last_pair]
    return (
        block_output,
        input_grad,
        jnp.where(first_core, last_one[:, head_size], last_two[:, head_size]),
        in_order(*query_pair),
        in_order(last_one[:, :head_size], last_two[:, :head_size]),
        in_order(*out_pair),
        jnp.where(first_core, last_two[:, head_size], last_one[:, head_size]),
        jnp.where(first_core, wide_one, wide_two),
        jnp.where(first_core, wide_two, wide_one),
        in_order(*down_pair),
    )


def solution(mesh):
    in_specs = (
        P(None, "grp", "shard", None),
        P(None, "grp", None),
        P(None, "grp", None),
        P(None, "grp", None),
        P("shard"),
        P("shard", None),
        P("shard", None),
        P("shard", None),
        P("shard"),
        P("shard", None),
        P("shard", None),
        P("shard", None),
        P(None, "grp", "shard", None),
    )
    out_specs = (
        P(None, "grp", "shard", None),
        P(None, "grp", "shard", None),
        P("shard"),
        P("shard", None),
        P("shard", None),
        P("shard", None),
        P("shard"),
        P("shard", None),
        P("shard", None),
        P("shard", None),
    )
    return jax.shard_map(
        on_device, mesh=mesh, in_specs=in_specs, out_specs=out_specs, check_vma=False
    )
```

```python
import functools
import math

import jax
import jax.numpy as jnp
from jax import lax
from jax.experimental import pallas as pl
from jax.experimental.pallas import tpu as pltpu
from jax.sharding import PartitionSpec as P

epsilon = 1e-06
masked_out = -1e30
bf16 = jnp.bfloat16
f32 = jnp.float32
plane = 4
ring_order = (0, 1, 3, 2)


def rms_factor(values):
    return lax.rsqrt(jnp.mean(values * values, axis=-1, keepdims=True) + epsilon)


def product(first_op, second_op):
    return jnp.dot(first_op, second_op, preferred_element_type=f32)


def product_tn(first_op, second_op):
    return lax.dot_general(
        first_op, second_op, (((0,), (0,)), ((), ())), preferred_element_type=f32
    )


def product_nt(first_op, second_op):
    return lax.dot_general(
        first_op, second_op, (((1,), (1,)), ((), ())), preferred_element_type=f32
    )


def norm_backward(values, factor, gain, upstream):
    inner_mean = jnp.mean(gain * upstream * values, axis=-1, keepdims=True)
    return factor * gain * upstream - values * factor * factor * factor * inner_mean


def tie(*values):
    return lax.optimization_barrier(values)


def across(value, mask):
    count = lax.axis_size("shard")
    return lax.ppermute(value, "shard", [(i, i ^ mask) for i in range(count)])


def peer(value):
    count = lax.axis_size("grp")
    return lax.ppermute(value, "grp", [(i, i ^ 1) for i in range(count)])


def column_groups():
    count = lax.axis_size("shard")
    return [[a * plane + b for a in range(count // plane)] for b in range(plane)]


def gather_column(value):
    return lax.all_gather(
        value, "shard", axis=0, tiled=True, axis_index_groups=column_groups()
    )


def scatter_column(value):
    return lax.psum_scatter(
        value, "shard", scatter_dimension=0, tiled=True, axis_index_groups=column_groups()
    )


def double_column(value):
    held = value[None]
    while held.shape[0] < lax.axis_size("shard") // plane:
        got = across(held, held.shape[0] * plane)
        held = jnp.concatenate([held, got], axis=0)
    return held


def halve_column(held, *during):
    during = list(during)
    ready = ()
    while held.shape[0] > 1:
        size = held.shape[0] // 2
        got = across(held[size:], size * plane)
        if during:
            got, *ready = tie(got, *during.pop(0)(*ready))
        held = (held[:size].astype(f32) + got.astype(f32)).astype(bf16)
    for rest in during:
        ready = rest(*ready)
    return held[0], ready


def start_plane(value):
    return across(value, 1), across(value, 2)


def finish_plane(value, first, second):
    half = value.shape[0] // 2
    far_top = across(first[:half], 2)
    far_bottom = across(second[half:], 1)
    return value, first, second, far_top, far_bottom


def gather_plane(value):
    return finish_plane(value, *tie(*start_plane(value)))


def place_kernel(relative, place, own, first, second, far_top, far_bottom, out):
    half = far_top.shape[0]
    me = place[0]
    line = place[1] // plane if relative else 0
    for at in range(own.shape[0]):
        far = far_top[at : at + 1] if at < half else far_bottom[at - half : at - half + 1]
        blocks = (own[at : at + 1], first[at : at + 1], second[at : at + 1], far)
        for mask, block in enumerate(blocks):
            out[pl.ds(line ^ at, 1), pl.ds(me ^ mask, 1)] = block[:, None]


def place_plane(blocks, place, relative=False):
    lead, rows, width = blocks[0].shape
    vmem = pl.BlockSpec(memory_space=pltpu.VMEM)
    return pl.pallas_call(
        functools.partial(place_kernel, relative),
        out_shape=jax.ShapeDtypeStruct((lead, plane, rows, width), blocks[0].dtype),
        in_specs=[pl.BlockSpec(memory_space=pltpu.SMEM)] + [vmem] * 5,
        out_specs=vmem,
        cost_estimate=pl.CostEstimate(
            flops=0, transcendentals=0, bytes_accessed=4 * plane * lead * rows * width
        ),
        name="place_plane",
    )(place, *blocks)


def unshuffle(pieces, place, unit):
    rows, part = pieces[0].shape
    lead = part // unit
    vmem = pl.BlockSpec(memory_space=pltpu.VMEM)

    def kernel(place, p0, p1, p2, p3, out, natural):
        for mask, piece in enumerate((p0, p1, p2, p3)):
            natural[pl.ds(place[0] ^ mask, 1)] = piece[...].astype(f32)[None]
        columns = [
            natural[member][:, a * unit : (a + 1) * unit]
            for a in range(lead)
            for member in range(plane)
        ]
        out[...] = jnp.concatenate(columns, axis=1).astype(bf16)

    return pl.pallas_call(
        kernel,
        out_shape=jax.ShapeDtypeStruct((rows, plane * part), bf16),
        in_specs=[pl.BlockSpec(memory_space=pltpu.SMEM)] + [vmem] * 4,
        out_specs=vmem,
        scratch_shapes=[pltpu.VMEM((plane, rows, part), f32)],
        cost_estimate=pl.CostEstimate(
            flops=0, transcendentals=0, bytes_accessed=4 * plane * rows * part
        ),
        name="unshuffle",
    )(place, *pieces)


def pass_plane(x_keep, x_got, y_keep, y_got):
    x_pass, y_pass = tie(
        (x_keep[1].astype(f32) + x_got[1].astype(f32)).astype(bf16),
        (y_keep[1].astype(f32) + y_got[0].astype(f32)).astype(bf16),
    )
    return across(x_pass, 2), across(y_pass, 1)


def exchange_plane(x_send, x_keep, y_send, y_keep, during_first=(), during_second=()):
    x_got, y_got, *during_first = tie(across(x_send, 1), across(y_send, 2), *during_first)
    x_last, y_last = pass_plane(x_keep, x_got, y_keep, y_got)
    x_last, y_last, *during_second = tie(x_last, y_last, *during_second)
    return x_got, x_last, y_got, y_last, during_first, during_second


def split_kernel(place, *refs):
    *pairs, x_send, x_keep, y_send, y_keep = refs
    half = x_send.shape[1]
    for out, slot, mask, first in (
        (x_send, 0, 1, 0),
        (x_send, 1, 3, 0),
        (x_keep, 0, 0, 0),
        (x_keep, 1, 2, 0),
        (y_send, 0, 3, half),
        (y_send, 1, 2, half),
        (y_keep, 0, 0, half),
        (y_keep, 1, 1, half),
    ):
        at = (slice(first, first + half), pl.ds(place[0] ^ mask, 1))
        start = 0
        for own, got in zip(pairs[::2], pairs[1::2]):
            end = start + own.shape[3]
            total = (own[at].astype(f32) + got[at].astype(f32))[:, 0].astype(bf16)
            out[slot, :, :, start:end] = total
            start = end


def split_rows(place, rows, *pairs):
    lead = pairs[0].shape[0] // (plane * rows)
    width = sum(value.shape[1] for value in pairs) // 2
    vmem = pl.BlockSpec(memory_space=pltpu.VMEM)
    sent = jax.ShapeDtypeStruct((2, lead // 2, rows, width), bf16)
    size = width * pairs[0].shape[0]
    return pl.pallas_call(
        split_kernel,
        out_shape=(sent,) * 4,
        in_specs=[pl.BlockSpec(memory_space=pltpu.SMEM)] + [vmem] * len(pairs),
        out_specs=(vmem,) * 4,
        cost_estimate=pl.CostEstimate(flops=size, transcendentals=0, bytes_accessed=6 * size),
        compiler_params=pltpu.CompilerParams(vmem_limit_bytes=56 * 2**20),
        name="split_rows",
    )(place, *(value.reshape(lead, plane, rows, value.shape[1]) for value in pairs))


def joined(x_keep, x_got, x_last, y_keep, y_got, y_last, axis):
    return jnp.concatenate(
        [
            x_keep[0].astype(f32) + x_got[0].astype(f32) + x_last.astype(f32),
            y_keep[0].astype(f32) + y_got[1].astype(f32) + y_last.astype(f32),
        ],
        axis=axis,
    ).astype(bf16)


def window_mask(info, dims, micro, piece):
    sub, window, keys, pad, seqs = dims
    base = piece * window + info[1] * sub
    query = base + lax.broadcasted_iota(jnp.int32, (sub, 1), 0)
    start = jnp.zeros((sub, 1), jnp.int32)
    end = jnp.int32(0)
    for k in range(seqs - 1):
        end = end + info[2 + micro * seqs + k]
        start = jnp.where(query >= end, end, start)
    lowest = jnp.maximum(start, query - (window - 1))
    key = base - pad + lax.broadcasted_iota(jnp.int32, (sub, keys), 1)
    return jnp.where((key >= lowest) & (key <= query), 0.0, masked_out).astype(f32)


def fill_window(info, dims, micro_count, pieces, blocks, key_all, value_all):
    sub, window, keys, pad, seqs = dims
    head_size = key_all.shape[-1]
    key_all[:, :pad, :] = jnp.zeros((micro_count, pad, head_size), bf16)
    value_all[:, :pad, :] = jnp.zeros((micro_count, pad, head_size), bf16)
    slots = micro_count * pieces
    offset = {0: 0, 1: 0, 2: 0, 3: 0}
    for mask, block in zip((0, 1, 2, 3, 3), blocks):
        member = info[0] ^ mask
        first = offset[mask]
        amount = block.shape[0] // sub

        def copy(step, carry, block=block, member=member, first=first):
            index = step + first
            row = pl.multiple_of(
                pad + (index % pieces) * window + ((index // slots) * plane + member) * sub, 16
            )
            micro = (index // pieces) % micro_count
            rows = block[pl.ds(pl.multiple_of(step * sub, 16), sub), :]
            key_all[micro, pl.ds(row, sub), :] = rows[:, :head_size]
            value_all[micro, pl.ds(row, sub), :] = rows[:, head_size:]
            return carry

        lax.fori_loop(0, amount, copy, 0)
        offset[mask] = first + amount


def stack_heads(ref, rows, heads, head_size):
    block = ref[rows, :]
    return jnp.concatenate(
        [block[:, h * head_size : (h + 1) * head_size] for h in heads], axis=0
    )


def attend_forward_kernel(
    dims, micro_count, pieces, group, info, q_ref, k0, k1, k2, k3, k4, o_ref, lse_ref, key_all, value_all
):
    sub, window, keys, pad, seqs = dims
    head_size = key_all.shape[-1]
    head_count = q_ref.shape[1] // head_size
    fill_window(info, dims, micro_count, pieces, (k0, k1, k2, k3, k4), key_all, value_all)
    scale = 1.0 / math.sqrt(head_size) / math.log(2.0)

    def slot(index, carry):
        micro = index // pieces
        piece = index % pieces
        bias = window_mask(info, dims, micro, piece)
        start = pl.multiple_of(piece * window + info[1] * sub, 16)
        key_part = key_all[micro, pl.ds(start, keys), :]
        value_part = value_all[micro, pl.ds(start, keys), :]
        rows = pl.ds(pl.multiple_of(index * sub, 16), sub)
        for first in range(0, head_count, group):
            heads = range(first, first + group)
            queries = stack_heads(q_ref, rows, heads, head_size)
            scores = product_nt(queries, key_part) * scale
            scores = scores.reshape(group, sub, keys) + bias[None]
            scores = scores.reshape(group * sub, keys)
            top = jnp.max(scores, axis=-1, keepdims=True)
            weights = jnp.exp2(scores - top)
            total = jnp.sum(weights, axis=-1, keepdims=True)
            mixed = (product(weights.astype(bf16), value_part) / total).astype(bf16)
            for at, h in enumerate(heads):
                o_ref[rows, h * head_size : (h + 1) * head_size] = mixed[at * sub : (at + 1) * sub]
            lse_ref[index, first * sub : (first + group) * sub, :] = top + jnp.log2(total)
        return carry

    lax.fori_loop(0, micro_count * pieces, slot, 0)


def attend_backward_kernel(
    dims,
    micro_count,
    pieces,
    group,
    info,
    q_ref,
    g_ref,
    lse_ref,
    k0,
    k1,
    k2,
    k3,
    k4,
    dq_ref,
    kx_send,
    kx_keep,
    vy_send,
    vy_keep,
    key_all,
    value_all,
    dkey_all,
    dvalue_all,
):
    sub, window, keys, pad, seqs = dims
    head_size = key_all.shape[-1]
    head_count = q_ref.shape[1] // head_size
    fill_window(info, dims, micro_count, pieces, (k0, k1, k2, k3, k4), key_all, value_all)
    dkey_all[...] = jnp.zeros(dkey_all.shape, f32)
    dvalue_all[...] = jnp.zeros(dvalue_all.shape, f32)
    plain = 1.0 / math.sqrt(head_size)
    scale = plain / math.log(2.0)

    def slot(index, carry):
        micro = index // pieces
        piece = index % pieces
        bias = window_mask(info, dims, micro, piece)
        start = pl.multiple_of(piece * window + info[1] * sub, 16)
        key_part = key_all[micro, pl.ds(start, keys), :]
        value_part = value_all[micro, pl.ds(start, keys), :]
        rows = pl.ds(pl.multiple_of(index * sub, 16), sub)
        dkey = jnp.zeros((keys, head_size), f32)
        dvalue = jnp.zeros((keys, head_size), f32)
        for first in range(0, head_count, group):
            heads = range(first, first + group)
            queries = stack_heads(q_ref, rows, heads, head_size)
            grads = stack_heads(g_ref, rows, heads, head_size)
            lse = lse_ref[index, first * sub : (first + group) * sub, :]
            scores = product_nt(queries, key_part) * scale
            scores = scores.reshape(group, sub, keys) + bias[None]
            prob = jnp.exp2(scores.reshape(group * sub, keys) - lse)
            dprob = product_nt(grads, value_part)
            delta = jnp.sum(prob * dprob, axis=-1, keepdims=True)
            dscore = (prob * (dprob - delta)).astype(bf16)
            dquery = (product(dscore, key_part) * plain).astype(bf16)
            for at, h in enumerate(heads):
                dq_ref[rows, h * head_size : (h + 1) * head_size] = dquery[
                    at * sub : (at + 1) * sub
                ]
            dkey = dkey + product_tn(dscore, queries)
            dvalue = dvalue + product_tn(prob.astype(bf16), grads)
        dkey_all[micro, pl.ds(start, keys), :] += dkey * plain
        dvalue_all[micro, pl.ds(start, keys), :] += dvalue
        return carry

    lax.fori_loop(0, micro_count * pieces, slot, 0)
    slots = micro_count * pieces
    line = info[1] // plane
    for mask, k_out, k_at, v_out, v_at in (
        (0, kx_keep, 0, vy_keep, 0),
        (1, kx_send, 0, vy_keep, 1),
        (2, kx_keep, 1, vy_send, 1),
        (3, kx_send, 1, vy_send, 0),
    ):
        member = info[0] ^ mask

        def copy(index, carry, member=member, k_out=k_out, k_at=k_at, v_out=v_out, v_at=v_at):
            row = pl.multiple_of(
                pad + (index % pieces) * window + (((index // slots) ^ line) * plane + member) * sub, 16
            )
            micro = (index // pieces) % micro_count
            to = pl.ds(pl.multiple_of(index * sub, 16), sub)
            k_out[k_at, to, :] = dkey_all[micro, pl.ds(row, sub), :].astype(bf16)
            v_out[v_at, to, :] = dvalue_all[micro, pl.ds(row, sub), :].astype(bf16)
            return carry

        lax.fori_loop(0, kx_keep.shape[1] // sub, copy, 0)


def attention_calls(micro_count, pieces, sub, window, head_size, head_count, seqs, kv_rows):
    keys = -(-(window + sub) // 128) * 128
    pad = keys - sub
    dims = (sub, window, keys, pad, seqs)
    group = max(g for g in range(1, head_count + 1) if head_count % g == 0 and g * sub <= max(384, sub))
    token_count = micro_count * pieces * sub
    width = head_count * head_size
    smem = pl.BlockSpec(memory_space=pltpu.SMEM)
    vmem = pl.BlockSpec(memory_space=pltpu.VMEM)
    shape = jax.ShapeDtypeStruct
    span = pad + pieces * window
    work = token_count * head_count * keys
    lse_shape = shape((micro_count * pieces, head_count * sub, 1), f32)
    params = pltpu.CompilerParams(vmem_limit_bytes=56 * 2**20)
    forward = pl.pallas_call(
        functools.partial(attend_forward_kernel, dims, micro_count, pieces, group),
        out_shape=(shape((token_count, width), bf16), lse_shape),
        in_specs=[smem] + [vmem] * 6,
        out_specs=(vmem, vmem),
        scratch_shapes=[pltpu.VMEM((micro_count, span, head_size), bf16)] * 2,
        cost_estimate=pl.CostEstimate(
            flops=4 * work * head_size, transcendentals=work, bytes_accessed=4 * 2**20
        ),
        compiler_params=params,
        name="attend_forward",
    )
    block = shape((2, kv_rows, head_size), bf16)
    backward = pl.pallas_call(
        functools.partial(attend_backward_kernel, dims, micro_count, pieces, group),
        out_shape=(shape((token_count, width), bf16), block, block, block, block),
        in_specs=[smem] + [vmem] * 8,
        out_specs=(vmem,) * 5,
        scratch_shapes=[pltpu.VMEM((micro_count, span, head_size), bf16)] * 2
        + [pltpu.VMEM((micro_count, span, head_size), f32)] * 2,
        cost_estimate=pl.CostEstimate(
            flops=10 * work * head_size, transcendentals=work, bytes_accessed=8 * 2**20
        ),
        compiler_params=params,
        name="attend_backward",
    )
    return forward, backward


def outproj_kernel(core, att, own, other, tokens, gain, residual, normed):
    half = own.shape[1]
    columns = (pl.ds(pl.multiple_of(core[0] * half, 128), half), pl.ds(pl.multiple_of((1 - core[0]) * half, 128), half))
    rows = att[...]
    for weight, cols in zip((own, other), columns):
        residual[:, cols] = product(rows, weight[...])
    total = residual[...] + tokens[...].astype(f32)
    residual[...] = total
    normed[...] = (total * rms_factor(total) * gain[...]).astype(bf16)


def outproj_norm(core, attended, own, other, tokens, gain):
    rows, width = tokens.shape
    vmem = pl.BlockSpec(memory_space=pltpu.VMEM)
    shape = jax.ShapeDtypeStruct
    return pl.pallas_call(
        outproj_kernel,
        out_shape=(shape((rows, width), f32), shape((rows, width), bf16)),
        in_specs=[pl.BlockSpec(memory_space=pltpu.SMEM)] + [vmem] * 5,
        out_specs=(vmem, vmem),
        cost_estimate=pl.CostEstimate(
            flops=2 * rows * width * attended.shape[1],
            transcendentals=0,
            bytes_accessed=2 * width * attended.shape[1] + 10 * rows * width,
        ),
        compiler_params=pltpu.CompilerParams(vmem_limit_bytes=56 * 2**20),
        name="outproj_norm",
    )(core, attended, own, other, tokens, gain)


def feed_kernel(
    core, h0, h1, h2, h3, h4, c0, c1, c2, c3, c4, w_own, w_other, d_own, d_other,
    h_all, c_all, hidden, g_own, g_other, x_send, x_keep, y_send, y_keep, total,
):
    rows = h0.shape[0]
    cut = rows // 2
    for out, blocks in ((h_all, (h0, h1, h3, h4, h2)), (c_all, (c0, c1, c3, c4, c2))):
        at = 0
        for block in blocks:
            out[at : at + block.shape[0], :] = block[...]
            at += block.shape[0]
    half = d_own.shape[1]
    part = hidden.shape[1]
    step = 384 if part % 384 == 0 else part
    is_first = core[0] == 0
    mine = pl.ds(pl.multiple_of(core[0] * half, 128), half)
    theirs = pl.ds(pl.multiple_of((1 - core[0]) * half, 128), half)
    root = math.sqrt(2.0 / math.pi)

    def block(index, carry):
        at = pl.ds(pl.multiple_of(index * rows, 16), rows)
        tokens = h_all[at, :]
        up_mine = c_all[at, mine]
        up_theirs = c_all[at, theirs]
        for first in range(0, part, step):
            cols = slice(first, first + step)
            pre_own = product(tokens, w_own[:, cols])
            pre_other = product(tokens, w_other[:, cols])
            gate = jnp.where(is_first, pre_own, pre_other)
            upward = jnp.where(is_first, pre_other, pre_own)
            grad = product_nt(up_mine, d_own[cols, :]) + product_nt(up_theirs, d_other[cols, :])
            square = gate * gate
            curve = jnp.tanh(root * gate * (1.0 + 0.044715 * square))
            lift = 0.5 * (1.0 + curve)
            active = gate * lift
            slope = lift + (0.5 * root) * gate * (1.0 - curve * curve) * (
                1.0 + (3 * 0.044715) * square
            )
            hidden[at, cols] = (active * upward).astype(bf16)
            grad_gate = grad * upward * slope
            grad_up = grad * active
            mine_in = jnp.where(is_first, grad_gate, grad_up).astype(bf16)
            theirs_in = jnp.where(is_first, grad_up, grad_gate).astype(bf16)
            g_own[at, cols] = mine_in
            g_other[at, cols] = theirs_in
            back = product_nt(mine_in, w_own[:, cols]) + product_nt(theirs_in, w_other[:, cols])
            if first == 0:
                total[at, :] = back
            else:
                total[at, :] += back
        return carry

    lax.fori_loop(0, plane, block, 0)
    width = total.shape[1] // 2
    for out, slot, member in (
        (x_keep, 0, 0), (x_send, 0, 1), (x_send, 1, 2), (x_keep, 1, 3),
    ):
        out[slot] = total[member * rows : (member + 1) * rows, :width].astype(bf16)
    for out, slot, member in (
        (y_keep, 0, 0), (y_keep, 1, 1), (y_send, 0, 2), (y_send, 1, 3),
    ):
        out[slot] = total[member * rows : (member + 1) * rows, width:].astype(bf16)


def feed_forward(core, h_blocks, c_blocks, w_own, w_other, d_own, d_other):
    rows, width = h_blocks[0].shape
    part = w_own.shape[1]
    count = plane * rows
    vmem = pl.BlockSpec(memory_space=pltpu.VMEM)
    shape = jax.ShapeDtypeStruct
    wide = shape((count, part), bf16)
    sent = shape((2, rows, width // 2), bf16)
    return pl.pallas_call(
        feed_kernel,
        out_shape=(shape((count, width), bf16),) * 2 + (wide,) * 3 + (sent,) * 4,
        in_specs=[pl.BlockSpec(memory_space=pltpu.SMEM)] + [vmem] * 14,
        out_specs=(vmem,) * 9,
        scratch_shapes=[pltpu.VMEM((count, width), f32)],
        cost_estimate=pl.CostEstimate(
            flops=10 * count * width * part,
            transcendentals=count * part,
            bytes_accessed=8 * width * part + 12 * count * part,
        ),
        compiler_params=pltpu.CompilerParams(vmem_limit_bytes=58 * 2**20),
        name="feed_forward",
    )(core, *h_blocks, *c_blocks, w_own, w_other, d_own, d_other)


def norm_two_kernel(
    core, x_keep, x_got, x_last, y_keep, y_got, y_last, residual, up, gain, own, other,
    grad_out, attn, mixed, grad_gain,
):
    width = x_last.shape[1]
    half = own.shape[1]
    mine = pl.ds(pl.multiple_of(core[0] * half, 128), half)
    theirs = pl.ds(pl.multiple_of((1 - core[0]) * half, 128), half)
    upstream = jnp.concatenate(
        [
            x_keep[0].astype(f32) + x_got[0].astype(f32) + x_last[...].astype(f32),
            y_keep[0].astype(f32) + y_got[1].astype(f32) + y_last[...].astype(f32),
        ],
        axis=1,
    )
    values = residual[...]
    factor = rms_factor(values)
    grad_gain[...] = jnp.sum(upstream * values * factor, axis=0, keepdims=True)
    total = up[...].astype(f32) + norm_backward(values, factor, gain[...], upstream)
    grad_out[...] = total
    attn[...] = total.astype(bf16)
    mixed[...] = (
        product_nt(attn[:, mine], own[...]) + product_nt(attn[:, theirs], other[...])
    ).astype(bf16)


def norm_two_backward(core, sums, residual, up, gain, own, other):
    rows, width = residual.shape
    vmem = pl.BlockSpec(memory_space=pltpu.VMEM)
    shape = jax.ShapeDtypeStruct
    return pl.pallas_call(
        norm_two_kernel,
        out_shape=(
            shape((rows, width), f32),
            shape((rows, width), bf16),
            shape((rows, own.shape[0]), bf16),
            shape((1, width), f32),
        ),
        in_specs=[pl.BlockSpec(memory_space=pltpu.SMEM)] + [vmem] * 11,
        out_specs=(vmem,) * 4,
        cost_estimate=pl.CostEstimate(
            flops=2 * rows * width * own.shape[0],
            transcendentals=0,
            bytes_accessed=2 * width * own.shape[0] + 20 * rows * width,
        ),
        compiler_params=pltpu.CompilerParams(vmem_limit_bytes=56 * 2**20),
        name="norm_two_backward",
    )(core, *sums, residual, up, gain, own, other)


def input_kernel(
    core, partial, dkv, kv_own, kv_other, normed, tokens, gain, other_gain, grad_resid,
    grad_input, last_own, last_other,
):
    head = kv_own.shape[1]
    mine = pl.ds(pl.multiple_of(core[0] * head, 128), head)
    theirs = pl.ds(pl.multiple_of((1 - core[0]) * head, 128), head)
    is_first = core[0] == 0
    upstream = (
        partial[...]
        + product_nt(dkv[:, mine], kv_own[...])
        + product_nt(dkv[:, theirs], kv_other[...])
    )
    values = tokens[...].astype(f32)
    factor = rms_factor(values)
    grad_gain = jnp.sum(upstream * values * factor, axis=0, keepdims=True)
    grad_input[...] = (
        grad_resid[...] + norm_backward(values, factor, gain[...], upstream)
    ).astype(bf16)
    kept = jnp.where(is_first, grad_gain, other_gain[...])
    given = jnp.where(is_first, other_gain[...], grad_gain)
    width = kept.shape[1]
    for out, cols, row in ((last_own, mine, kept), (last_other, theirs, given)):
        out[:, :head] = product_tn(normed[...], dkv[:, cols]).astype(bf16)
        out[:, head:] = jnp.broadcast_to(row, (128, width)).T.astype(bf16)


def input_backward(core, partial, dkv, kv_own, kv_other, normed, tokens, gain, other_gain, grad_resid):
    rows, width = tokens.shape
    vmem = pl.BlockSpec(memory_space=pltpu.VMEM)
    shape = jax.ShapeDtypeStruct
    last = shape((width, kv_own.shape[1] + 128), bf16)
    return pl.pallas_call(
        input_kernel,
        out_shape=(shape((rows, width), bf16), last, last),
        in_specs=[pl.BlockSpec(memory_space=pltpu.SMEM)] + [vmem] * 9,
        out_specs=(vmem,) * 3,
        cost_estimate=pl.CostEstimate(
            flops=8 * rows * width * kv_own.shape[1],
            transcendentals=0,
            bytes_accessed=16 * rows * width,
        ),
        compiler_params=pltpu.CompilerParams(vmem_limit_bytes=56 * 2**20),
        name="input_backward",
    )(core, partial, dkv, kv_own, kv_other, normed, tokens, gain, other_gain, grad_resid)


def on_device(
    tokens,
    lengths,
    piece_order,
    predecessor,
    gain_one,
    query_weight,
    keyval_weight,
    outproj_weight,
    gain_two,
    gate_weight,
    up_weight,
    down_weight,
    cotangent,
):
    shard_count = lax.axis_size("shard")
    grp_count = lax.axis_size("grp")
    lead = shard_count // plane
    micro_count, piece_count, sub_rows, feat = tokens.shape
    window = sub_rows * shard_count
    token_count = micro_count * piece_count * sub_rows
    head_size = keyval_weight.shape[1] // 2
    width = query_weight.shape[1]
    head_count = width // head_size
    hidden_width = gate_weight.shape[1]
    my_rows = query_weight.shape[0]
    my_hidden = down_weight.shape[0]
    part = hidden_width // plane
    half_w = width // 2
    half_d = feat // 2
    my_index = lax.axis_index("shard")
    my_place = my_index % plane
    core = lax.axis_index("grp") % 2
    first_core = core == 0

    def in_order(own, other):
        return jnp.where(
            first_core,
            jnp.concatenate([own, other], axis=1),
            jnp.concatenate([other, own], axis=1),
        )

    def halves(value):
        size = value.shape[1] // 2
        return (
            lax.dynamic_slice_in_dim(value, core * size, size, 1),
            lax.dynamic_slice_in_dim(value, (1 - core) * size, size, 1),
        )

    place = jnp.stack([my_place, my_index]).astype(jnp.int32)

    def by_lead(value):
        return value.reshape(lead, my_rows, -1)

    def plane_weight(blocks):
        return place_plane(blocks, place).reshape(feat, -1)

    qo_line = gather_column(
        jnp.concatenate([halves(query_weight)[0], halves(outproj_weight)[0]], axis=1)
    )
    gain_cols = jnp.pad(jnp.stack([gain_one, gain_two], axis=1), ((0, 0), (0, 126)))
    kv_mine = jnp.concatenate([halves(keyval_weight)[0], gain_cols], axis=1)
    kv_line = gather_column(kv_mine)
    upstream = cotangent.reshape(token_count, feat)
    gate_or_up = jnp.where(first_core, gate_weight, up_weight)
    up_first, up_second, kv_line, gate_or_up = tie(
        *start_plane(upstream), by_lead(kv_line), gate_or_up
    )
    pieces_out = jnp.transpose(
        gate_or_up.reshape(my_rows, lead, plane, my_hidden), (2, 0, 1, 3)
    ).reshape(plane, my_rows, part)
    wide_in = jnp.zeros((plane, my_rows, part), bf16)
    for mask in range(plane):
        block = lax.dynamic_index_in_dim(pieces_out, my_place ^ mask, axis=0, keepdims=True)
        block = block if mask == 0 else across(block, mask)
        wide_in = lax.dynamic_update_slice_in_dim(wide_in, block, my_place ^ mask, axis=0)
    kv_own = plane_weight(gather_plane(kv_line))
    kv_own, qo_line = tie(kv_own, qo_line)
    query_line, out_line = by_lead(qo_line[:, :half_w]), by_lead(qo_line[:, half_w:])
    query_first, query_second = start_plane(query_line)
    out_first, out_second = start_plane(out_line)
    kv_other = peer(kv_own)
    gains = kv_own[:, head_size : head_size + 2].T
    kv_own, kv_other = kv_own[:, :head_size], kv_other[:, :head_size]
    full_gain_one = gains[0].astype(f32)
    full_gain_two = gains[1].astype(f32)

    stream = tokens.reshape(token_count, feat).astype(f32)
    factor_one = rms_factor(stream)
    normed_one = (stream * factor_one * full_gain_one).astype(bf16)
    keyvals = in_order(product(normed_one, kv_own), product(normed_one, kv_other)).astype(bf16)
    keyvals, wide_in = tie(keyvals, wide_in)
    wide_own = gather_column(wide_in.reshape(plane * my_rows, part))
    down_own = gather_column(halves(down_weight)[0])
    keyvals_line, query_first, query_second, out_first, out_second = tie(
        gather_column(keyvals), query_first, query_second, out_first, out_second
    )
    query_blocks = finish_plane(query_line, query_first, query_second)
    key_first, key_second, *query_blocks = tie(*start_plane(keyvals_line), *query_blocks)
    query_own = plane_weight(query_blocks)
    kv_blocks = finish_plane(keyvals_line, key_first, key_second)
    out_blocks = finish_plane(out_line, out_first, out_second)
    *blocks, query_own = tie(*kv_blocks, *out_blocks, query_own)
    kv_blocks, out_blocks = blocks[:5], blocks[5:]
    out_own = plane_weight(out_blocks)
    query_other = peer(query_own)
    out_other = peer(out_own)
    queries = in_order(product(normed_one, query_own), product(normed_one, query_other)).astype(bf16)
    forward, backward = attention_calls(
        micro_count,
        piece_count,
        sub_rows,
        window,
        head_size,
        head_count,
        lengths.shape[-1],
        lead * token_count,
    )
    info = jnp.concatenate([place, lengths.reshape(-1).astype(jnp.int32)])
    attended, logsum = forward(info, queries, *kv_blocks)
    attended, *up_blocks = tie(attended, *finish_plane(upstream, up_first, up_second))
    core_info = core.astype(jnp.int32).reshape(1)
    gain_two_row = full_gain_two.reshape(1, feat)
    residual, normed_two = outproj_norm(
        core_info,
        attended,
        out_own,
        out_other,
        tokens.reshape(token_count, feat),
        gain_two_row,
    )

    normed_first, normed_second, wide_own, down_own = tie(
        *start_plane(normed_two), wide_own, down_own
    )
    normed_blocks = finish_plane(normed_two, normed_first, normed_second)
    wide_other = peer(wide_own)
    down_other = peer(down_own)
    all_normed, all_up, hidden, grad_own_in, grad_other_in, *sums = feed_forward(
        core_info, normed_blocks, up_blocks, wide_own, wide_other, down_own, down_other
    )
    up_own, up_other = halves(all_up)

    def chip_sum(own, other):
        return (own.astype(f32) + peer(other.astype(bf16)).astype(f32)).astype(bf16)

    wide_peer = product_tn(all_normed, grad_other_in).astype(bf16)
    wide_mine = product_tn(all_normed, grad_own_in).astype(bf16)
    x_send, x_keep, y_send, y_keep = sums
    x_got, y_got, wide_mine, wide_peer = tie(
        across(x_send, 1), across(y_send, 2), wide_mine, wide_peer
    )
    x_pass, y_pass, wide_mine, wide_peer, hidden = tie(
        (x_keep[1].astype(f32) + x_got[1].astype(f32)).astype(bf16),
        (y_keep[1].astype(f32) + y_got[0].astype(f32)).astype(bf16),
        wide_mine,
        wide_peer,
        hidden,
    )
    x_last, y_last, out_mine, out_peer, wide_sum = tie(
        across(x_pass, 2),
        across(y_pass, 1),
        product(hidden, down_own).astype(bf16),
        product(hidden, down_other).astype(bf16),
        chip_sum(wide_mine, wide_peer),
    )
    wide_grad = scatter_column(wide_sum)
    grad_resid, grad_attn, grad_mixed, grad_gain_two = norm_two_backward(
        core_info,
        (x_keep, x_got, x_last, y_keep, y_got, y_last),
        residual,
        upstream,
        gain_two_row,
        out_own,
        out_other,
    )

    one = out_mine.reshape(plane, token_count, -1)
    two = out_peer.reshape(plane, token_count, -1)
    grad_queries, kx_send, kx_keep, vy_send, vy_keep = backward(
        info, queries, grad_mixed, logsum, *kv_blocks
    )
    out_x, out_y, grad_queries, kx_send, kx_keep, vy_send, vy_keep, grad_attn, hidden = tie(
        across(one[1:3], 1),
        across(two[2:4], 2),
        grad_queries,
        kx_send,
        kx_keep,
        vy_send,
        vy_keep,
        grad_attn,
        hidden,
    )
    dq_own, dq_other = halves(grad_queries)
    da_own, da_other = halves(grad_attn)
    attn_mine = product_tn(attended, da_own).astype(bf16)
    attn_peer = peer(product_tn(attended, da_other).astype(bf16))
    kx_got, vy_got, attn_mine, attn_peer, query_mine, query_peer = tie(
        across(kx_send, 1),
        across(vy_send, 2),
        attn_mine,
        attn_peer,
        product_tn(normed_one, dq_own).astype(bf16),
        peer(product_tn(normed_one, dq_other).astype(bf16)),
    )
    kx_last, vy_last = pass_plane(kx_keep, kx_got, vy_keep, vy_got)
    kx_last, vy_last, hidden, attn_x, attn_x_keep, attn_y, attn_y_keep = tie(
        kx_last,
        vy_last,
        hidden,
        *split_rows(place, my_rows, query_mine, query_peer, attn_mine, attn_peer),
    )
    attn_x, attn_y = across(attn_x, 1), across(attn_y, 2)
    grad_kv, wide_grad = tie(
        joined(kx_keep, kx_got, kx_last, vy_keep, vy_got, vy_last, 1), wide_grad
    )
    partial = product_nt(dq_own, query_own) + product_nt(dq_other, query_other)

    def first_step():
        return (
            product_tn(hidden, up_own).astype(bf16),
            peer(product_tn(hidden, up_other).astype(bf16)),
        )

    def second_step(down_mine, down_peer):
        down_sum = (down_mine.astype(f32) + down_peer.astype(f32)).astype(bf16)
        return partial, down_sum, attn_x, attn_y

    grad_keyvals, (partial, down_sum, attn_x, attn_y) = halve_column(
        grad_kv.reshape(lead, token_count, -1), first_step, second_step
    )
    down_grad = scatter_column(down_sum)
    wide_grad = wide_grad.reshape(plane, my_rows, part)
    input_grad, last_own, last_other = input_backward(
        core_info,
        partial,
        grad_keyvals,
        kv_own,
        kv_other,
        normed_one,
        tokens.reshape(token_count, feat),
        full_gain_one.reshape(1, feat),
        grad_gain_two,
        grad_resid,
    )
    input_grad = input_grad.reshape(tokens.shape)
    last_split = split_rows(place, my_rows, last_own, peer(last_other))
    attn_x_last, attn_y_last = pass_plane(attn_x_keep, attn_x, attn_y_keep, attn_y)
    attn_plane = joined(
        attn_x_keep, attn_x, attn_x_last, attn_y_keep, attn_y, attn_y_last, 0
    ).reshape(lead * my_rows, -1)
    last_x, last_x_keep, last_y, last_y_keep = last_split
    last_x, last_x_last, last_y, last_y_last, _, _ = exchange_plane(
        last_x, last_x_keep, last_y, last_y_keep
    )
    last_plane = joined(
        last_x_keep, last_x, last_x_last, last_y_keep, last_y, last_y_last, 0
    ).reshape(lead * my_rows, -1)
    last_plane, down_grad, out_x, out_y = tie(last_plane, down_grad, out_x, out_y)
    last_share = scatter_column(
        jnp.concatenate([attn_plane, last_plane], axis=1)
    )

    out_x_last, out_y_last = pass_plane((one[0], one[3]), out_x, (two[0], two[1]), out_y)
    out_sum = (
        one[0].astype(f32) + out_x[0].astype(f32) + out_x_last.astype(f32),
        two[0].astype(f32) + out_y[1].astype(f32) + out_y_last.astype(f32),
    )
    block_output = (residual + in_order(*out_sum)).astype(bf16).reshape(tokens.shape)

    wide_back = []
    for mask in range(plane):
        block = lax.dynamic_index_in_dim(wide_grad, my_place ^ mask, axis=0, keepdims=False)
        wide_back.append(block if mask == 0 else across(block, mask))
    wide_share = unshuffle(wide_back, place, my_hidden)

    def whole(share):
        total = share
        for step in range(1, grp_count // 2):
            moved = lax.ppermute(
                share, "grp", [(i, (i + 2 * step) % grp_count) for i in range(grp_count)]
            )
            total = total.astype(f32) + moved.astype(f32)
        total = total.astype(bf16)
        return total.astype(f32), peer(total).astype(f32)

    wide_one, wide_two = whole(wide_share)
    down_pair = whole(down_grad)
    last_pair = whole(last_share)
    query_pair = [share[:, :half_w] for share in last_pair]
    out_pair = [share[:, half_w : half_w + half_d] for share in last_pair]
    last_one, last_two = [share[:, half_w + half_d :] for share in last_pair]
    return (
        block_output,
        input_grad,
        jnp.where(first_core, last_one[:, head_size], last_two[:, head_size]),
        in_order(*query_pair),
        in_order(last_one[:, :head_size], last_two[:, :head_size]),
        in_order(*out_pair),
        jnp.where(first_core, last_two[:, head_size], last_one[:, head_size]),
        jnp.where(first_core, wide_one, wide_two),
        jnp.where(first_core, wide_two, wide_one),
        in_order(*down_pair),
    )


def solution(mesh):
    in_specs = (
        P(None, "grp", "shard", None),
        P(None, "grp", None),
        P(None, "grp", None),
        P(None, "grp", None),
        P("shard"),
        P("shard", None),
        P("shard", None),
        P("shard", None),
        P("shard"),
        P("shard", None),
        P("shard", None),
        P("shard", None),
        P(None, "grp", "shard", None),
    )
    out_specs = (
        P(None, "grp", "shard", None),
        P(None, "grp", "shard", None),
        P("shard"),
        P("shard", None),
        P("shard", None),
        P("shard", None),
        P("shard"),
        P("shard", None),
        P("shard", None),
        P("shard", None),
    )
    return jax.shard_map(
        on_device, mesh=mesh, in_specs=in_specs, out_specs=out_specs, check_vma=False
    )
```

```python
import functools
import math

import jax
import jax.numpy as jnp
from jax import lax
from jax.experimental import pallas as pl
from jax.experimental.pallas import tpu as pltpu
from jax.sharding import PartitionSpec as P

epsilon = 1e-06
masked_out = -1e30
bf16 = jnp.bfloat16
f32 = jnp.float32
plane = 4
ring_order = (0, 1, 3, 2)


def rms_factor(values):
    return lax.rsqrt(jnp.mean(values * values, axis=-1, keepdims=True) + epsilon)


def product(first_op, second_op):
    return jnp.dot(first_op, second_op, preferred_element_type=f32)


def product_tn(first_op, second_op):
    return lax.dot_general(
        first_op, second_op, (((0,), (0,)), ((), ())), preferred_element_type=f32
    )


def product_nt(first_op, second_op):
    return lax.dot_general(
        first_op, second_op, (((1,), (1,)), ((), ())), preferred_element_type=f32
    )


def norm_backward(values, factor, gain, upstream):
    inner_mean = jnp.mean(gain * upstream * values, axis=-1, keepdims=True)
    return factor * gain * upstream - values * factor * factor * factor * inner_mean


def tie(*values):
    return lax.optimization_barrier(values)


def across(value, mask):
    count = lax.axis_size("shard")
    return lax.ppermute(value, "shard", [(i, i ^ mask) for i in range(count)])


def peer(value):
    count = lax.axis_size("grp")
    return lax.ppermute(value, "grp", [(i, i ^ 1) for i in range(count)])


def column_groups():
    count = lax.axis_size("shard")
    return [[a * plane + b for a in range(count // plane)] for b in range(plane)]


def gather_column(value):
    return lax.all_gather(
        value, "shard", axis=0, tiled=True, axis_index_groups=column_groups()
    )


def scatter_column(value):
    return lax.psum_scatter(
        value, "shard", scatter_dimension=0, tiled=True, axis_index_groups=column_groups()
    )


def double_column(value):
    held = value[None]
    while held.shape[0] < lax.axis_size("shard") // plane:
        got = across(held, held.shape[0] * plane)
        held = jnp.concatenate([held, got], axis=0)
    return held


def halve_column(held, *during):
    during = list(during)
    ready = ()
    while held.shape[0] > 1:
        size = held.shape[0] // 2
        got = across(held[size:], size * plane)
        if during:
            got, *ready = tie(got, *during.pop(0)(*ready))
        held = (held[:size].astype(f32) + got.astype(f32)).astype(bf16)
    for rest in during:
        ready = rest(*ready)
    return held[0], ready


def start_plane(value):
    return across(value, 1), across(value, 2)


def finish_plane(value, first, second):
    half = value.shape[0] // 2
    far_top = across(first[:half], 2)
    far_bottom = across(second[half:], 1)
    return value, first, second, far_top, far_bottom


def gather_plane(value):
    return finish_plane(value, *tie(*start_plane(value)))


def place_kernel(relative, place, own, first, second, far_top, far_bottom, out):
    half = far_top.shape[0]
    me = place[0]
    line = place[1] // plane if relative else 0
    for at in range(own.shape[0]):
        far = far_top[at : at + 1] if at < half else far_bottom[at - half : at - half + 1]
        blocks = (own[at : at + 1], first[at : at + 1], second[at : at + 1], far)
        for mask, block in enumerate(blocks):
            out[pl.ds(line ^ at, 1), pl.ds(me ^ mask, 1)] = block[:, None]


def place_plane(blocks, place, relative=False):
    lead, rows, width = blocks[0].shape
    vmem = pl.BlockSpec(memory_space=pltpu.VMEM)
    return pl.pallas_call(
        functools.partial(place_kernel, relative),
        out_shape=jax.ShapeDtypeStruct((lead, plane, rows, width), blocks[0].dtype),
        in_specs=[pl.BlockSpec(memory_space=pltpu.SMEM)] + [vmem] * 5,
        out_specs=vmem,
        cost_estimate=pl.CostEstimate(
            flops=0, transcendentals=0, bytes_accessed=4 * plane * lead * rows * width
        ),
        name="place_plane",
    )(place, *blocks)


def unshuffle(pieces, place, unit):
    rows, part = pieces[0].shape
    lead = part // unit
    vmem = pl.BlockSpec(memory_space=pltpu.VMEM)

    def kernel(place, p0, p1, p2, p3, out, natural):
        for mask, piece in enumerate((p0, p1, p2, p3)):
            natural[pl.ds(place[0] ^ mask, 1)] = piece[...].astype(f32)[None]
        columns = [
            natural[member][:, a * unit : (a + 1) * unit]
            for a in range(lead)
            for member in range(plane)
        ]
        out[...] = jnp.concatenate(columns, axis=1).astype(bf16)

    return pl.pallas_call(
        kernel,
        out_shape=jax.ShapeDtypeStruct((rows, plane * part), bf16),
        in_specs=[pl.BlockSpec(memory_space=pltpu.SMEM)] + [vmem] * 4,
        out_specs=vmem,
        scratch_shapes=[pltpu.VMEM((plane, rows, part), f32)],
        cost_estimate=pl.CostEstimate(
            flops=0, transcendentals=0, bytes_accessed=4 * plane * rows * part
        ),
        name="unshuffle",
    )(place, *pieces)


def pass_plane(x_keep, x_got, y_keep, y_got):
    x_pass, y_pass = tie(
        (x_keep[1].astype(f32) + x_got[1].astype(f32)).astype(bf16),
        (y_keep[1].astype(f32) + y_got[0].astype(f32)).astype(bf16),
    )
    return across(x_pass, 2), across(y_pass, 1)


def exchange_plane(x_send, x_keep, y_send, y_keep, during_first=(), during_second=()):
    x_got, y_got, *during_first = tie(across(x_send, 1), across(y_send, 2), *during_first)
    x_last, y_last = pass_plane(x_keep, x_got, y_keep, y_got)
    x_last, y_last, *during_second = tie(x_last, y_last, *during_second)
    return x_got, x_last, y_got, y_last, during_first, during_second


def split_kernel(place, *refs):
    *pairs, x_send, x_keep, y_send, y_keep = refs
    half = x_send.shape[1]
    for out, slot, mask, first in (
        (x_send, 0, 1, 0),
        (x_send, 1, 3, 0),
        (x_keep, 0, 0, 0),
        (x_keep, 1, 2, 0),
        (y_send, 0, 3, half),
        (y_send, 1, 2, half),
        (y_keep, 0, 0, half),
        (y_keep, 1, 1, half),
    ):
        at = (slice(first, first + half), pl.ds(place[0] ^ mask, 1))
        start = 0
        for own, got in zip(pairs[::2], pairs[1::2]):
            end = start + own.shape[3]
            total = (own[at].astype(f32) + got[at].astype(f32))[:, 0].astype(bf16)
            out[slot, :, :, start:end] = total
            start = end


def split_rows(place, rows, *pairs):
    lead = pairs[0].shape[0] // (plane * rows)
    width = sum(value.shape[1] for value in pairs) // 2
    vmem = pl.BlockSpec(memory_space=pltpu.VMEM)
    sent = jax.ShapeDtypeStruct((2, lead // 2, rows, width), bf16)
    size = width * pairs[0].shape[0]
    return pl.pallas_call(
        split_kernel,
        out_shape=(sent,) * 4,
        in_specs=[pl.BlockSpec(memory_space=pltpu.SMEM)] + [vmem] * len(pairs),
        out_specs=(vmem,) * 4,
        cost_estimate=pl.CostEstimate(flops=size, transcendentals=0, bytes_accessed=6 * size),
        compiler_params=pltpu.CompilerParams(vmem_limit_bytes=56 * 2**20),
        name="split_rows",
    )(place, *(value.reshape(lead, plane, rows, value.shape[1]) for value in pairs))


def joined(x_keep, x_got, x_last, y_keep, y_got, y_last, axis):
    return jnp.concatenate(
        [
            x_keep[0].astype(f32) + x_got[0].astype(f32) + x_last.astype(f32),
            y_keep[0].astype(f32) + y_got[1].astype(f32) + y_last.astype(f32),
        ],
        axis=axis,
    ).astype(bf16)


def window_mask(info, dims, micro, piece):
    sub, window, keys, pad, seqs = dims
    base = piece * window + info[1] * sub
    query = base + lax.broadcasted_iota(jnp.int32, (sub, 1), 0)
    start = jnp.zeros((sub, 1), jnp.int32)
    end = jnp.int32(0)
    for k in range(seqs - 1):
        end = end + info[2 + micro * seqs + k]
        start = jnp.where(query >= end, end, start)
    lowest = jnp.maximum(start, query - (window - 1))
    key = base - pad + lax.broadcasted_iota(jnp.int32, (sub, keys), 1)
    return jnp.where((key >= lowest) & (key <= query), 0.0, masked_out).astype(f32)


def fill_window(info, dims, micro_count, pieces, blocks, key_all, value_all):
    sub, window, keys, pad, seqs = dims
    head_size = key_all.shape[-1]
    key_all[:, :pad, :] = jnp.zeros((micro_count, pad, head_size), bf16)
    value_all[:, :pad, :] = jnp.zeros((micro_count, pad, head_size), bf16)
    slots = micro_count * pieces
    offset = {0: 0, 1: 0, 2: 0, 3: 0}
    for mask, block in zip((0, 1, 2, 3, 3), blocks):
        member = info[0] ^ mask
        first = offset[mask]
        amount = block.shape[0] // sub

        def copy(step, carry, block=block, member=member, first=first):
            index = step + first
            row = pl.multiple_of(
                pad + (index % pieces) * window + ((index // slots) * plane + member) * sub, 16
            )
            micro = (index // pieces) % micro_count
            rows = block[pl.ds(pl.multiple_of(step * sub, 16), sub), :]
            key_all[micro, pl.ds(row, sub), :] = rows[:, :head_size]
            value_all[micro, pl.ds(row, sub), :] = rows[:, head_size:]
            return carry

        lax.fori_loop(0, amount, copy, 0)
        offset[mask] = first + amount


def stack_heads(ref, rows, heads, head_size):
    block = ref[rows, :]
    return jnp.concatenate(
        [block[:, h * head_size : (h + 1) * head_size] for h in heads], axis=0
    )


def attend_forward_kernel(
    dims, micro_count, pieces, group, info, q_ref, k0, k1, k2, k3, k4, o_ref, lse_ref, key_all, value_all
):
    sub, window, keys, pad, seqs = dims
    head_size = key_all.shape[-1]
    head_count = q_ref.shape[1] // head_size
    fill_window(info, dims, micro_count, pieces, (k0, k1, k2, k3, k4), key_all, value_all)
    scale = 1.0 / math.sqrt(head_size) / math.log(2.0)

    def slot(index, carry):
        micro = index // pieces
        piece = index % pieces
        bias = window_mask(info, dims, micro, piece)
        start = pl.multiple_of(piece * window + info[1] * sub, 16)
        key_part = key_all[micro, pl.ds(start, keys), :]
        value_part = value_all[micro, pl.ds(start, keys), :]
        rows = pl.ds(pl.multiple_of(index * sub, 16), sub)
        for first in range(0, head_count, group):
            heads = range(first, first + group)
            queries = stack_heads(q_ref, rows, heads, head_size)
            scores = product_nt(queries, key_part) * scale
            scores = scores.reshape(group, sub, keys) + bias[None]
            scores = scores.reshape(group * sub, keys)
            top = jnp.max(scores, axis=-1, keepdims=True)
            weights = jnp.exp2(scores - top)
            total = jnp.sum(weights, axis=-1, keepdims=True)
            mixed = (product(weights.astype(bf16), value_part) / total).astype(bf16)
            for at, h in enumerate(heads):
                o_ref[rows, h * head_size : (h + 1) * head_size] = mixed[at * sub : (at + 1) * sub]
            lse_ref[index, first * sub : (first + group) * sub, :] = top + jnp.log2(total)
        return carry

    lax.fori_loop(0, micro_count * pieces, slot, 0)


def attend_backward_kernel(
    dims,
    micro_count,
    pieces,
    group,
    info,
    q_ref,
    g_ref,
    lse_ref,
    k0,
    k1,
    k2,
    k3,
    k4,
    dq_ref,
    kx_send,
    kx_keep,
    vy_send,
    vy_keep,
    key_all,
    value_all,
    dkey_all,
    dvalue_all,
):
    sub, window, keys, pad, seqs = dims
    head_size = key_all.shape[-1]
    head_count = q_ref.shape[1] // head_size
    fill_window(info, dims, micro_count, pieces, (k0, k1, k2, k3, k4), key_all, value_all)
    dkey_all[...] = jnp.zeros(dkey_all.shape, f32)
    dvalue_all[...] = jnp.zeros(dvalue_all.shape, f32)
    plain = 1.0 / math.sqrt(head_size)
    scale = plain / math.log(2.0)

    def slot(index, carry):
        micro = index // pieces
        piece = index % pieces
        bias = window_mask(info, dims, micro, piece)
        start = pl.multiple_of(piece * window + info[1] * sub, 16)
        key_part = key_all[micro, pl.ds(start, keys), :]
        value_part = value_all[micro, pl.ds(start, keys), :]
        rows = pl.ds(pl.multiple_of(index * sub, 16), sub)
        dkey = jnp.zeros((keys, head_size), f32)
        dvalue = jnp.zeros((keys, head_size), f32)
        for first in range(0, head_count, group):
            heads = range(first, first + group)
            queries = stack_heads(q_ref, rows, heads, head_size)
            grads = stack_heads(g_ref, rows, heads, head_size)
            lse = lse_ref[index, first * sub : (first + group) * sub, :]
            scores = product_nt(queries, key_part) * scale
            scores = scores.reshape(group, sub, keys) + bias[None]
            prob = jnp.exp2(scores.reshape(group * sub, keys) - lse)
            dprob = product_nt(grads, value_part)
            delta = jnp.sum(prob * dprob, axis=-1, keepdims=True)
            dscore = (prob * (dprob - delta)).astype(bf16)
            dquery = (product(dscore, key_part) * plain).astype(bf16)
            for at, h in enumerate(heads):
                dq_ref[rows, h * head_size : (h + 1) * head_size] = dquery[
                    at * sub : (at + 1) * sub
                ]
            dkey = dkey + product_tn(dscore, queries)
            dvalue = dvalue + product_tn(prob.astype(bf16), grads)
        dkey_all[micro, pl.ds(start, keys), :] += dkey * plain
        dvalue_all[micro, pl.ds(start, keys), :] += dvalue
        return carry

    lax.fori_loop(0, micro_count * pieces, slot, 0)
    slots = micro_count * pieces
    line = info[1] // plane
    for mask, k_out, k_at, v_out, v_at in (
        (0, kx_keep, 0, vy_keep, 0),
        (1, kx_send, 0, vy_keep, 1),
        (2, kx_keep, 1, vy_send, 1),
        (3, kx_send, 1, vy_send, 0),
    ):
        member = info[0] ^ mask

        def copy(index, carry, member=member, k_out=k_out, k_at=k_at, v_out=v_out, v_at=v_at):
            row = pl.multiple_of(
                pad + (index % pieces) * window + (((index // slots) ^ line) * plane + member) * sub, 16
            )
            micro = (index // pieces) % micro_count
            to = pl.ds(pl.multiple_of(index * sub, 16), sub)
            k_out[k_at, to, :] = dkey_all[micro, pl.ds(row, sub), :].astype(bf16)
            v_out[v_at, to, :] = dvalue_all[micro, pl.ds(row, sub), :].astype(bf16)
            return carry

        lax.fori_loop(0, kx_keep.shape[1] // sub, copy, 0)


def attention_calls(micro_count, pieces, sub, window, head_size, head_count, seqs, kv_rows):
    keys = -(-(window + sub) // 128) * 128
    pad = keys - sub
    dims = (sub, window, keys, pad, seqs)
    group = max(g for g in range(1, head_count + 1) if head_count % g == 0 and g * sub <= max(384, sub))
    token_count = micro_count * pieces * sub
    width = head_count * head_size
    smem = pl.BlockSpec(memory_space=pltpu.SMEM)
    vmem = pl.BlockSpec(memory_space=pltpu.VMEM)
    shape = jax.ShapeDtypeStruct
    span = pad + pieces * window
    work = token_count * head_count * keys
    lse_shape = shape((micro_count * pieces, head_count * sub, 1), f32)
    params = pltpu.CompilerParams(vmem_limit_bytes=56 * 2**20)
    forward = pl.pallas_call(
        functools.partial(attend_forward_kernel, dims, micro_count, pieces, group),
        out_shape=(shape((token_count, width), bf16), lse_shape),
        in_specs=[smem] + [vmem] * 6,
        out_specs=(vmem, vmem),
        scratch_shapes=[pltpu.VMEM((micro_count, span, head_size), bf16)] * 2,
        cost_estimate=pl.CostEstimate(
            flops=4 * work * head_size, transcendentals=work, bytes_accessed=4 * 2**20
        ),
        compiler_params=params,
        name="attend_forward",
    )
    block = shape((2, kv_rows, head_size), bf16)
    backward = pl.pallas_call(
        functools.partial(attend_backward_kernel, dims, micro_count, pieces, group),
        out_shape=(shape((token_count, width), bf16), block, block, block, block),
        in_specs=[smem] + [vmem] * 8,
        out_specs=(vmem,) * 5,
        scratch_shapes=[pltpu.VMEM((micro_count, span, head_size), bf16)] * 2
        + [pltpu.VMEM((micro_count, span, head_size), f32)] * 2,
        cost_estimate=pl.CostEstimate(
            flops=10 * work * head_size, transcendentals=work, bytes_accessed=8 * 2**20
        ),
        compiler_params=params,
        name="attend_backward",
    )
    return forward, backward


def outproj_kernel(core, att, own, other, tokens, gain, residual, normed):
    half = own.shape[1]
    columns = (pl.ds(pl.multiple_of(core[0] * half, 128), half), pl.ds(pl.multiple_of((1 - core[0]) * half, 128), half))
    rows = att[...]
    for weight, cols in zip((own, other), columns):
        residual[:, cols] = product(rows, weight[...])
    total = residual[...] + tokens[...].astype(f32)
    residual[...] = total
    normed[...] = (total * rms_factor(total) * gain[...]).astype(bf16)


def outproj_norm(core, attended, own, other, tokens, gain):
    rows, width = tokens.shape
    vmem = pl.BlockSpec(memory_space=pltpu.VMEM)
    shape = jax.ShapeDtypeStruct
    return pl.pallas_call(
        outproj_kernel,
        out_shape=(shape((rows, width), f32), shape((rows, width), bf16)),
        in_specs=[pl.BlockSpec(memory_space=pltpu.SMEM)] + [vmem] * 5,
        out_specs=(vmem, vmem),
        cost_estimate=pl.CostEstimate(
            flops=2 * rows * width * attended.shape[1],
            transcendentals=0,
            bytes_accessed=2 * width * attended.shape[1] + 10 * rows * width,
        ),
        compiler_params=pltpu.CompilerParams(vmem_limit_bytes=56 * 2**20),
        name="outproj_norm",
    )(core, attended, own, other, tokens, gain)


def feed_kernel(
    core, h0, h1, h2, h3, h4, c0, c1, c2, c3, c4, w_own, w_other, d_own, d_other,
    h_all, c_all, hidden, g_own, g_other, x_send, x_keep, y_send, y_keep, total,
):
    rows = h0.shape[0]
    cut = rows // 2
    for out, blocks in ((h_all, (h0, h1, h3, h4, h2)), (c_all, (c0, c1, c3, c4, c2))):
        at = 0
        for block in blocks:
            out[at : at + block.shape[0], :] = block[...]
            at += block.shape[0]
    half = d_own.shape[1]
    part = hidden.shape[1]
    step = 384 if part % 384 == 0 else part
    is_first = core[0] == 0
    mine = pl.ds(pl.multiple_of(core[0] * half, 128), half)
    theirs = pl.ds(pl.multiple_of((1 - core[0]) * half, 128), half)
    root = math.sqrt(2.0 / math.pi)

    def block(index, carry):
        at = pl.ds(pl.multiple_of(index * rows, 16), rows)
        tokens = h_all[at, :]
        up_mine = c_all[at, mine]
        up_theirs = c_all[at, theirs]
        for first in range(0, part, step):
            cols = slice(first, first + step)
            pre_own = product(tokens, w_own[:, cols])
            pre_other = product(tokens, w_other[:, cols])
            gate = jnp.where(is_first, pre_own, pre_other)
            upward = jnp.where(is_first, pre_other, pre_own)
            grad = product_nt(up_mine, d_own[cols, :]) + product_nt(up_theirs, d_other[cols, :])
            square = gate * gate
            curve = jnp.tanh(root * gate * (1.0 + 0.044715 * square))
            lift = 0.5 * (1.0 + curve)
            active = gate * lift
            slope = lift + (0.5 * root) * gate * (1.0 - curve * curve) * (
                1.0 + (3 * 0.044715) * square
            )
            hidden[at, cols] = (active * upward).astype(bf16)
            grad_gate = grad * upward * slope
            grad_up = grad * active
            mine_in = jnp.where(is_first, grad_gate, grad_up).astype(bf16)
            theirs_in = jnp.where(is_first, grad_up, grad_gate).astype(bf16)
            g_own[at, cols] = mine_in
            g_other[at, cols] = theirs_in
            back = product_nt(mine_in, w_own[:, cols]) + product_nt(theirs_in, w_other[:, cols])
            if first == 0:
                total[at, :] = back
            else:
                total[at, :] += back
        return carry

    lax.fori_loop(0, plane, block, 0)
    width = total.shape[1] // 2
    for out, slot, member in (
        (x_keep, 0, 0), (x_send, 0, 1), (x_send, 1, 2), (x_keep, 1, 3),
    ):
        out[slot] = total[member * rows : (member + 1) * rows, :width].astype(bf16)
    for out, slot, member in (
        (y_keep, 0, 0), (y_keep, 1, 1), (y_send, 0, 2), (y_send, 1, 3),
    ):
        out[slot] = total[member * rows : (member + 1) * rows, width:].astype(bf16)


def feed_forward(core, h_blocks, c_blocks, w_own, w_other, d_own, d_other):
    rows, width = h_blocks[0].shape
    part = w_own.shape[1]
    count = plane * rows
    vmem = pl.BlockSpec(memory_space=pltpu.VMEM)
    shape = jax.ShapeDtypeStruct
    wide = shape((count, part), bf16)
    sent = shape((2, rows, width // 2), bf16)
    return pl.pallas_call(
        feed_kernel,
        out_shape=(shape((count, width), bf16),) * 2 + (wide,) * 3 + (sent,) * 4,
        in_specs=[pl.BlockSpec(memory_space=pltpu.SMEM)] + [vmem] * 14,
        out_specs=(vmem,) * 9,
        scratch_shapes=[pltpu.VMEM((count, width), f32)],
        cost_estimate=pl.CostEstimate(
            flops=10 * count * width * part,
            transcendentals=count * part,
            bytes_accessed=8 * width * part + 12 * count * part,
        ),
        compiler_params=pltpu.CompilerParams(vmem_limit_bytes=58 * 2**20),
        name="feed_forward",
    )(core, *h_blocks, *c_blocks, w_own, w_other, d_own, d_other)


def norm_two_kernel(
    core, x_keep, x_got, x_last, y_keep, y_got, y_last, residual, up, gain, own, other,
    grad_out, attn, mixed, grad_gain,
):
    width = x_last.shape[1]
    half = own.shape[1]
    mine = pl.ds(pl.multiple_of(core[0] * half, 128), half)
    theirs = pl.ds(pl.multiple_of((1 - core[0]) * half, 128), half)
    upstream = jnp.concatenate(
        [
            x_keep[0].astype(f32) + x_got[0].astype(f32) + x_last[...].astype(f32),
            y_keep[0].astype(f32) + y_got[1].astype(f32) + y_last[...].astype(f32),
        ],
        axis=1,
    )
    values = residual[...]
    factor = rms_factor(values)
    grad_gain[...] = jnp.sum(upstream * values * factor, axis=0, keepdims=True)
    total = up[...].astype(f32) + norm_backward(values, factor, gain[...], upstream)
    grad_out[...] = total
    attn[...] = total.astype(bf16)
    mixed[...] = (
        product_nt(attn[:, mine], own[...]) + product_nt(attn[:, theirs], other[...])
    ).astype(bf16)


def norm_two_backward(core, sums, residual, up, gain, own, other):
    rows, width = residual.shape
    vmem = pl.BlockSpec(memory_space=pltpu.VMEM)
    shape = jax.ShapeDtypeStruct
    return pl.pallas_call(
        norm_two_kernel,
        out_shape=(
            shape((rows, width), f32),
            shape((rows, width), bf16),
            shape((rows, own.shape[0]), bf16),
            shape((1, width), f32),
        ),
        in_specs=[pl.BlockSpec(memory_space=pltpu.SMEM)] + [vmem] * 11,
        out_specs=(vmem,) * 4,
        cost_estimate=pl.CostEstimate(
            flops=2 * rows * width * own.shape[0],
            transcendentals=0,
            bytes_accessed=2 * width * own.shape[0] + 20 * rows * width,
        ),
        compiler_params=pltpu.CompilerParams(vmem_limit_bytes=56 * 2**20),
        name="norm_two_backward",
    )(core, *sums, residual, up, gain, own, other)


def input_kernel(
    core, partial, dkv, kv_own, kv_other, normed, tokens, gain, other_gain, grad_resid,
    grad_input, last_own, last_other,
):
    head = kv_own.shape[1]
    mine = pl.ds(pl.multiple_of(core[0] * head, 128), head)
    theirs = pl.ds(pl.multiple_of((1 - core[0]) * head, 128), head)
    is_first = core[0] == 0
    upstream = (
        partial[...]
        + product_nt(dkv[:, mine], kv_own[...])
        + product_nt(dkv[:, theirs], kv_other[...])
    )
    values = tokens[...].astype(f32)
    factor = rms_factor(values)
    grad_gain = jnp.sum(upstream * values * factor, axis=0, keepdims=True)
    grad_input[...] = (
        grad_resid[...] + norm_backward(values, factor, gain[...], upstream)
    ).astype(bf16)
    kept = jnp.where(is_first, grad_gain, other_gain[...])
    given = jnp.where(is_first, other_gain[...], grad_gain)
    width = kept.shape[1]
    for out, cols, row in ((last_own, mine, kept), (last_other, theirs, given)):
        out[:, :head] = product_tn(normed[...], dkv[:, cols]).astype(bf16)
        out[:, head:] = jnp.broadcast_to(row, (128, width)).T.astype(bf16)


def input_backward(core, partial, dkv, kv_own, kv_other, normed, tokens, gain, other_gain, grad_resid):
    rows, width = tokens.shape
    vmem = pl.BlockSpec(memory_space=pltpu.VMEM)
    shape = jax.ShapeDtypeStruct
    last = shape((width, kv_own.shape[1] + 128), bf16)
    return pl.pallas_call(
        input_kernel,
        out_shape=(shape((rows, width), bf16), last, last),
        in_specs=[pl.BlockSpec(memory_space=pltpu.SMEM)] + [vmem] * 9,
        out_specs=(vmem,) * 3,
        cost_estimate=pl.CostEstimate(
            flops=8 * rows * width * kv_own.shape[1],
            transcendentals=0,
            bytes_accessed=16 * rows * width,
        ),
        compiler_params=pltpu.CompilerParams(vmem_limit_bytes=56 * 2**20),
        name="input_backward",
    )(core, partial, dkv, kv_own, kv_other, normed, tokens, gain, other_gain, grad_resid)


def on_device(
    tokens,
    lengths,
    piece_order,
    predecessor,
    gain_one,
    query_weight,
    keyval_weight,
    outproj_weight,
    gain_two,
    gate_weight,
    up_weight,
    down_weight,
    cotangent,
):
    shard_count = lax.axis_size("shard")
    grp_count = lax.axis_size("grp")
    lead = shard_count // plane
    micro_count, piece_count, sub_rows, feat = tokens.shape
    window = sub_rows * shard_count
    token_count = micro_count * piece_count * sub_rows
    head_size = keyval_weight.shape[1] // 2
    width = query_weight.shape[1]
    head_count = width // head_size
    hidden_width = gate_weight.shape[1]
    my_rows = query_weight.shape[0]
    my_hidden = down_weight.shape[0]
    part = hidden_width // plane
    half_w = width // 2
    half_d = feat // 2
    my_index = lax.axis_index("shard")
    my_place = my_index % plane
    core = lax.axis_index("grp") % 2
    first_core = core == 0

    def in_order(own, other):
        return jnp.where(
            first_core,
            jnp.concatenate([own, other], axis=1),
            jnp.concatenate([other, own], axis=1),
        )

    def halves(value):
        size = value.shape[1] // 2
        return (
            lax.dynamic_slice_in_dim(value, core * size, size, 1),
            lax.dynamic_slice_in_dim(value, (1 - core) * size, size, 1),
        )

    place = jnp.stack([my_place, my_index]).astype(jnp.int32)

    def by_lead(value):
        return value.reshape(lead, my_rows, -1)

    def plane_weight(blocks):
        return place_plane(blocks, place).reshape(feat, -1)

    qo_line = gather_column(
        jnp.concatenate([halves(query_weight)[0], halves(outproj_weight)[0]], axis=1)
    )
    gain_cols = jnp.pad(jnp.stack([gain_one, gain_two], axis=1), ((0, 0), (0, 126)))
    kv_mine = jnp.concatenate([halves(keyval_weight)[0], gain_cols], axis=1)
    kv_line = gather_column(kv_mine)
    upstream = cotangent.reshape(token_count, feat)
    gate_or_up = jnp.where(first_core, gate_weight, up_weight)
    up_first, up_second, kv_line, gate_or_up = tie(
        *start_plane(upstream), by_lead(kv_line), gate_or_up
    )
    pieces_out = jnp.transpose(
        gate_or_up.reshape(my_rows, lead, plane, my_hidden), (2, 0, 1, 3)
    ).reshape(plane, my_rows, part)
    wide_in = jnp.zeros((plane, my_rows, part), bf16)
    for mask in range(plane):
        block = lax.dynamic_index_in_dim(pieces_out, my_place ^ mask, axis=0, keepdims=True)
        block = block if mask == 0 else across(block, mask)
        wide_in = lax.dynamic_update_slice_in_dim(wide_in, block, my_place ^ mask, axis=0)
    kv_own = plane_weight(gather_plane(kv_line))
    kv_own, qo_line = tie(kv_own, qo_line)
    query_line, out_line = by_lead(qo_line[:, :half_w]), by_lead(qo_line[:, half_w:])
    query_first, query_second = start_plane(query_line)
    out_first, out_second = start_plane(out_line)
    kv_other = peer(kv_own)
    gains = kv_own[:, head_size : head_size + 2].T
    kv_own, kv_other = kv_own[:, :head_size], kv_other[:, :head_size]
    full_gain_one = gains[0].astype(f32)
    full_gain_two = gains[1].astype(f32)

    stream = tokens.reshape(token_count, feat).astype(f32)
    factor_one = rms_factor(stream)
    normed_one = (stream * factor_one * full_gain_one).astype(bf16)
    keyvals = in_order(product(normed_one, kv_own), product(normed_one, kv_other)).astype(bf16)
    keyvals, wide_in = tie(keyvals, wide_in)
    wide_own = gather_column(wide_in.reshape(plane * my_rows, part))
    down_own = gather_column(halves(down_weight)[0])
    keyvals_line, query_first, query_second, out_first, out_second = tie(
        gather_column(keyvals), query_first, query_second, out_first, out_second
    )
    query_blocks = finish_plane(query_line, query_first, query_second)
    key_first, key_second, *query_blocks = tie(*start_plane(keyvals_line), *query_blocks)
    query_own = plane_weight(query_blocks)
    kv_blocks = finish_plane(keyvals_line, key_first, key_second)
    out_blocks = finish_plane(out_line, out_first, out_second)
    *blocks, query_own = tie(*kv_blocks, *out_blocks, query_own)
    kv_blocks, out_blocks = blocks[:5], blocks[5:]
    out_own = plane_weight(out_blocks)
    query_other = peer(query_own)
    out_other = peer(out_own)
    queries = in_order(product(normed_one, query_own), product(normed_one, query_other)).astype(bf16)
    forward, backward = attention_calls(
        micro_count,
        piece_count,
        sub_rows,
        window,
        head_size,
        head_count,
        lengths.shape[-1],
        lead * token_count,
    )
    info = jnp.concatenate([place, lengths.reshape(-1).astype(jnp.int32)])
    attended, logsum = forward(info, queries, *kv_blocks)
    attended, *up_blocks = tie(attended, *finish_plane(upstream, up_first, up_second))
    core_info = core.astype(jnp.int32).reshape(1)
    gain_two_row = full_gain_two.reshape(1, feat)
    residual, normed_two = outproj_norm(
        core_info,
        attended,
        out_own,
        out_other,
        tokens.reshape(token_count, feat),
        gain_two_row,
    )

    normed_first, normed_second, wide_own, down_own = tie(
        *start_plane(normed_two), wide_own, down_own
    )
    normed_blocks = finish_plane(normed_two, normed_first, normed_second)
    wide_other = peer(wide_own)
    down_other = peer(down_own)
    all_normed, all_up, hidden, grad_own_in, grad_other_in, *sums = feed_forward(
        core_info, normed_blocks, up_blocks, wide_own, wide_other, down_own, down_other
    )
    up_own, up_other = halves(all_up)

    def chip_sum(own, other):
        return (own.astype(f32) + peer(other.astype(bf16)).astype(f32)).astype(bf16)

    wide_peer = product_tn(all_normed, grad_other_in).astype(bf16)
    wide_mine = product_tn(all_normed, grad_own_in).astype(bf16)
    x_send, x_keep, y_send, y_keep = sums
    x_got, y_got, wide_mine, wide_peer = tie(
        across(x_send, 1), across(y_send, 2), wide_mine, wide_peer
    )
    x_pass, y_pass, wide_mine, wide_peer, hidden = tie(
        (x_keep[1].astype(f32) + x_got[1].astype(f32)).astype(bf16),
        (y_keep[1].astype(f32) + y_got[0].astype(f32)).astype(bf16),
        wide_mine,
        wide_peer,
        hidden,
    )
    x_last, y_last, out_mine, out_peer, wide_sum = tie(
        across(x_pass, 2),
        across(y_pass, 1),
        product(hidden, down_own).astype(bf16),
        product(hidden, down_other).astype(bf16),
        chip_sum(wide_mine, wide_peer),
    )
    wide_grad = scatter_column(wide_sum)
    grad_resid, grad_attn, grad_mixed, grad_gain_two = norm_two_backward(
        core_info,
        (x_keep, x_got, x_last, y_keep, y_got, y_last),
        residual,
        upstream,
        gain_two_row,
        out_own,
        out_other,
    )

    one = out_mine.reshape(plane, token_count, -1)
    two = out_peer.reshape(plane, token_count, -1)
    grad_queries, kx_send, kx_keep, vy_send, vy_keep = backward(
        info, queries, grad_mixed, logsum, *kv_blocks
    )
    out_x, out_y, grad_queries, kx_send, kx_keep, vy_send, vy_keep, grad_attn, hidden = tie(
        across(one[1:3], 1),
        across(two[2:4], 2),
        grad_queries,
        kx_send,
        kx_keep,
        vy_send,
        vy_keep,
        grad_attn,
        hidden,
    )
    dq_own, dq_other = halves(grad_queries)
    da_own, da_other = halves(grad_attn)
    attn_mine = product_tn(attended, da_own).astype(bf16)
    attn_peer = peer(product_tn(attended, da_other).astype(bf16))
    kx_got, vy_got, attn_mine, attn_peer, query_mine, query_peer = tie(
        across(kx_send, 1),
        across(vy_send, 2),
        attn_mine,
        attn_peer,
        product_tn(normed_one, dq_own).astype(bf16),
        peer(product_tn(normed_one, dq_other).astype(bf16)),
    )
    kx_last, vy_last = pass_plane(kx_keep, kx_got, vy_keep, vy_got)
    kx_last, vy_last, hidden, attn_x, attn_x_keep, attn_y, attn_y_keep = tie(
        kx_last,
        vy_last,
        hidden,
        *split_rows(place, my_rows, query_mine, query_peer, attn_mine, attn_peer),
    )
    attn_x, attn_y = across(attn_x, 1), across(attn_y, 2)
    grad_kv, wide_grad = tie(
        joined(kx_keep, kx_got, kx_last, vy_keep, vy_got, vy_last, 1), wide_grad
    )
    partial = product_nt(dq_own, query_own) + product_nt(dq_other, query_other)

    def first_step():
        return (
            product_tn(hidden, up_own).astype(bf16),
            product_tn(hidden, up_other).astype(bf16),
        )

    def second_step(down_mine, down_peer):
        return partial, down_mine, down_peer, attn_x, attn_y

    grad_keyvals, (partial, down_mine, down_peer, attn_x, attn_y) = halve_column(
        grad_kv.reshape(lead, token_count, -1), first_step, second_step
    )
    grad_keyvals, down_sum = tie(grad_keyvals, chip_sum(down_mine, down_peer))
    down_grad = scatter_column(down_sum)
    wide_grad = wide_grad.reshape(plane, my_rows, part)
    input_grad, last_own, last_other = input_backward(
        core_info,
        partial,
        grad_keyvals,
        kv_own,
        kv_other,
        normed_one,
        tokens.reshape(token_count, feat),
        full_gain_one.reshape(1, feat),
        grad_gain_two,
        grad_resid,
    )
    input_grad = input_grad.reshape(tokens.shape)
    last_split = split_rows(place, my_rows, last_own, peer(last_other))
    attn_x_last, attn_y_last = pass_plane(attn_x_keep, attn_x, attn_y_keep, attn_y)
    attn_plane = joined(
        attn_x_keep, attn_x, attn_x_last, attn_y_keep, attn_y, attn_y_last, 0
    ).reshape(lead * my_rows, -1)
    last_x, last_x_keep, last_y, last_y_keep = last_split
    last_x, last_x_last, last_y, last_y_last, _, _ = exchange_plane(
        last_x, last_x_keep, last_y, last_y_keep
    )
    last_plane = joined(
        last_x_keep, last_x, last_x_last, last_y_keep, last_y, last_y_last, 0
    ).reshape(lead * my_rows, -1)
    last_plane, down_grad, out_x, out_y = tie(last_plane, down_grad, out_x, out_y)
    last_share = scatter_column(
        jnp.concatenate([attn_plane, last_plane], axis=1)
    )

    out_x_last, out_y_last = pass_plane((one[0], one[3]), out_x, (two[0], two[1]), out_y)
    out_sum = (
        one[0].astype(f32) + out_x[0].astype(f32) + out_x_last.astype(f32),
        two[0].astype(f32) + out_y[1].astype(f32) + out_y_last.astype(f32),
    )
    block_output = (residual + in_order(*out_sum)).astype(bf16).reshape(tokens.shape)

    wide_back = []
    for mask in range(plane):
        block = lax.dynamic_index_in_dim(wide_grad, my_place ^ mask, axis=0, keepdims=False)
        wide_back.append(block if mask == 0 else across(block, mask))
    wide_share = unshuffle(wide_back, place, my_hidden)

    def whole(share):
        total = share
        for step in range(1, grp_count // 2):
            moved = lax.ppermute(
                share, "grp", [(i, (i + 2 * step) % grp_count) for i in range(grp_count)]
            )
            total = total.astype(f32) + moved.astype(f32)
        total = total.astype(bf16)
        return total.astype(f32), peer(total).astype(f32)

    wide_one, wide_two = whole(wide_share)
    down_pair = whole(down_grad)
    last_pair = whole(last_share)
    query_pair = [share[:, :half_w] for share in last_pair]
    out_pair = [share[:, half_w : half_w + half_d] for share in last_pair]
    last_one, last_two = [share[:, half_w + half_d :] for share in last_pair]
    return (
        block_output,
        input_grad,
        jnp.where(first_core, last_one[:, head_size], last_two[:, head_size]),
        in_order(*query_pair),
        in_order(last_one[:, :head_size], last_two[:, :head_size]),
        in_order(*out_pair),
        jnp.where(first_core, last_two[:, head_size], last_one[:, head_size]),
        jnp.where(first_core, wide_one, wide_two),
        jnp.where(first_core, wide_two, wide_one),
        in_order(*down_pair),
    )


def solution(mesh):
    in_specs = (
        P(None, "grp", "shard", None),
        P(None, "grp", None),
        P(None, "grp", None),
        P(None, "grp", None),
        P("shard"),
        P("shard", None),
        P("shard", None),
        P("shard", None),
        P("shard"),
        P("shard", None),
        P("shard", None),
        P("shard", None),
        P(None, "grp", "shard", None),
    )
    out_specs = (
        P(None, "grp", "shard", None),
        P(None, "grp", "shard", None),
        P("shard"),
        P("shard", None),
        P("shard", None),
        P("shard", None),
        P("shard"),
        P("shard", None),
        P("shard", None),
        P("shard", None),
    )
    return jax.shard_map(
        on_device, mesh=mesh, in_specs=in_specs, out_specs=out_specs, check_vma=False
    )
```
